32 devices in a mesh: head: 2 (over x), expert: 16 (over z, y, core).
Axes of the slice: x: 2, y: 2, z: 4, core: 2. Of those that a mesh axis runs over, the one named last changes fastest.
Arguments:
- queries: bfloat16 [256, 128, 576], P('expert', 'head'), may hold values from -64 to 64
- resident_cache: bfloat16 [64, 256, 576], P('expert'), may hold values from -6 to 6
- resident_len: int32 [64], P('expert'), may hold values from 1 to 256, as said below
- new_cache: bfloat16 [192, 64, 576], P('expert'), may hold values from -6 to 6
- new_len: int32 [192], replicated, may hold values from 1 to 64, as said below
- new_owner: int32 [192], replicated, may hold values from 0 to 15, as said below
- value_up: bfloat16 [128, 512, 128], P('head'), may hold values from -0.25 to 0.25
- w_output: bfloat16 [16384, 7168], P('head', 'expert'), may hold values from -0.046875 to 0.046875
- residual: bfloat16 [256, 7168], P(None, 'expert'), may hold values from -6 to 6
- expert_ids: int32 [256, 8], replicated, may hold values from 0 to 15, all different within a row; in each aligned block of 16 rows (0 to 15, 16 to 31, ...) at most 12 rows name the same one
- expert_gates: float32 [256, 8], replicated, may hold values from 0.1 to 1
- norm_gain: bfloat16 [7168], replicated, may hold values from 0.5 to 1.5
- w_gate: bfloat16 [16, 7168, 1024], P('expert', None, 'head'), may hold values from -0.0625 to 0.0625
- w_up: bfloat16 [16, 7168, 1024], P('expert', None, 'head'), may hold values from -0.0625 to 0.0625
- w_down: bfloat16 [16, 1024, 7168], P('expert', 'head'), may hold values from -0.1875 to 0.1875
Outputs:
- layer_out: bfloat16 [256, 7168], P('head', 'expert')
The draws below stay inside these ranges and needn't reach their ends.
Inputs may be any that keep to these rules, and one draw needn't show every extreme that they name: `resident_len`: every decode owner has a resident request of length 256. `new_len`: every prefill device holds a new request of length 64. `new_owner`: one prefill device sends at most 2 of its 12 new requests to one decode owner, and every decode owner receives exactly 12 in all; a prefill device sends either 2 or none to each owner, except to at most one owner, which gets the remainder of 12 divided by 2. `expert_ids`: in each aligned block of 16 rows (the rows of one decode owner) no expert is named by more than 12 rows; the 8 experts of a row differ.
All inputs are finite; a program needn't handle non-finite values.
Results may differ from the reference program's by a relative error of at most 0.012.
Values may be sent and summed in bfloat16 or wider, within the bound.
A program may use at most 128 MiB of HBM per device.

```python
import math
import jax
import jax.numpy as jnp
import numpy as np
from jax import lax

D = 7168
H = 128
LAT = 512
ROPE = 64
NOPE = 128
VDIM = 128
EFF = 1024
TOPK = 8
REQ_DEV = 4
CTX = 256
NEW_DEV = 12
NEWLEN = 64
EXPERTS = 16
ROWS_DEV = 16
ROWS = 256
REQS = 64
NEWS = 192
MOST = 2
CAP = 12
N_EXPERT = 16


def draw_queries(key, part):
    values = jax.random.normal(key, (ROWS, H, LAT + ROPE), jnp.float32)
    return jnp.clip(values, -64.0, 64.0).astype(jnp.bfloat16)


def draw_resident_len(key, part):
    base = jax.random.randint(key, (N_EXPERT, REQ_DEV), 1, CTX + 1)
    chosen = jax.random.randint(jax.random.fold_in(key, 3), (N_EXPERT, 1), 0, REQ_DEV)
    longest = jnp.arange(REQ_DEV)[None, :] == chosen
    return jnp.where(longest, CTX, base).reshape(REQS).astype(jnp.int32)


def draw_new_len(key, part):
    base = jax.random.randint(key, (N_EXPERT, NEW_DEV), 1, NEWLEN + 1)
    chosen = jax.random.randint(jax.random.fold_in(key, 5), (N_EXPERT, 1), 0, NEW_DEV)
    longest = jnp.arange(NEW_DEV)[None, :] == chosen
    return jnp.where(longest, NEWLEN, base).reshape(NEWS).astype(jnp.int32)


def draw_new_owner(key, part):
    spread = jax.random.permutation(jax.random.fold_in(key, 11), N_EXPERT)
    shifted = jax.random.permutation(jax.random.fold_in(key, 12), N_EXPERT)
    offsets = jax.random.permutation(jax.random.fold_in(key, 13), N_EXPERT)
    labels = jax.vmap(lambda one: jax.random.permutation(one, NEW_DEV))(jax.random.split(jax.random.fold_in(key, 14), N_EXPERT))
    groups = labels // MOST
    target = (shifted[:, None] + offsets[groups]) % N_EXPERT
    return spread[target].reshape(NEWS).astype(jnp.int32)


def level_of(own_key, shape, pieces, least, top_value):
    def one(position, shards_of):
        steps = jax.random.uniform(jax.random.fold_in(jax.random.fold_in(own_key, 6), position), (shards_of,), jnp.float32, least / len(pieces), top_value / len(pieces))
        return jnp.repeat(jnp.exp(steps), shape[position] // shards_of).reshape((-1,) + (1,) * (len(shape) - position - 1))

    level = one(*pieces[0])
    for cut in pieces[1:]:
        level = level * one(*cut)
    return level


def shared_out(own_key, own, number, rows, amount, top, limit, slope):
    order = jax.random.permutation(own_key, amount)
    crowded, usual = shares(amount, rows * top, limit, slope, True), shares(amount, rows * top, limit, slope, False)
    places = jnp.arange(amount)

    def named(lengths, offset_by):
        used = int((lengths > 0).sum())
        fixed = max(1, used // 4)
        moved = fixed + (places - fixed + offset_by * (used - fixed)) % max(1, amount - fixed)
        return jnp.zeros((amount,), jnp.int32).at[order[jnp.where(places < fixed, places, moved)]].set(jnp.asarray(lengths, jnp.int32))

    lengths = jnp.where(number % 4 == 0, named(crowded, number // 4), named(usual, number - number // 4 - 1))
    mixed = jax.random.permutation(jax.random.fold_in(own, 3), amount)
    source_of, receiver = mixed[0:amount // 2 * 2:2], mixed[1:amount // 2 * 2:2]
    margin = jnp.minimum(lengths[source_of] - 1, limit - lengths[receiver]) // 2
    margin = jnp.where((source_of == order[0]) | (receiver == order[0]) | (lengths[receiver] == 0), 0, jnp.maximum(margin, 0))
    moved = jax.random.randint(jax.random.fold_in(own, 4), (amount // 2,), 0, 1 << 20) % (margin + 1)
    lengths = lengths.at[source_of].add(-moved).at[receiver].add(moved)
    members = jnp.searchsorted(jnp.cumsum(lengths), jnp.arange(rows * top), side="right").astype(jnp.int32)
    grid = members.reshape(top, rows).T
    grid = grid[jax.random.permutation(jax.random.fold_in(own, 1), rows)]
    offset_by = jax.random.randint(jax.random.fold_in(own, 2), (rows, 1), 0, top)
    return jnp.take_along_axis(grid, (jnp.arange(top)[None, :] + offset_by) % top, axis=1)


def shares(amount, total, reach, slope, full):
    portions = [(1 << 20) // math.isqrt(grade ** slope) + 1 for grade in range(1, amount + 1)]
    largest = reach if full else min(reach, max(-(-total // amount), total * portions[0] // sum(portions)))
    least = 1 if total - largest >= amount - 1 else 0
    holding, rest = [largest] + [least] * (amount - 1), total - largest - least * (amount - 1)
    while rest > 0:
        candidates = [i for i in range(1, amount) if holding[i] < largest] or [i for i in range(1, amount) if holding[i] < reach]
        whole, left = sum([portions[i] for i in candidates]), rest
        for i in candidates:
            addition = min(reach - holding[i], max(1, left * portions[i] // whole), rest)
            holding[i] = holding[i] + addition
            rest = rest - addition
    return np.array(holding)


def noise(key, dims, width, limit, shards=(), kind=jnp.bfloat16):
    entries = width * jax.random.normal(key, dims, jnp.float32)
    if shards:
        entries = entries * level_of(key, dims, shards, -0.22, 0.18)
    return jnp.clip(entries, -limit, limit).astype(kind)


def setup_inputs(seed: int = 0) -> dict:
    key_list = jax.random.split(jax.random.key(seed), 16)
    queries = draw_queries(jax.random.fold_in(key_list[15], 71), 0)
    resident_cache = noise(key_list[1], (REQS, CTX, LAT + ROPE), 1.0, 6.0, ((0, 16),))
    resident_len = draw_resident_len(jax.random.fold_in(key_list[15], 71), 0)
    new_cache = noise(key_list[3], (NEWS, NEWLEN, LAT + ROPE), 1.0, 6.0, ((0, 16),))
    new_len = draw_new_len(jax.random.fold_in(key_list[15], 71), 0)
    new_owner = draw_new_owner(jax.random.fold_in(key_list[15], 71), 0)
    value_up = noise(key_list[6], (H, LAT, VDIM), LAT ** -0.5, 0.25, ((0, 2),))
    w_output = noise(key_list[7], (H * VDIM, D), (H * VDIM) ** -0.5, 0.046875, ((0, 2), (1, 16)))
    residual = noise(key_list[8], (ROWS, D), 1.0, 6.0, ((1, 16),))
    expert_ids_keys = jax.random.split(jax.random.fold_in(key_list[9], 1), ROWS // ROWS_DEV)
    expert_ids_turns = jax.random.permutation(jax.random.fold_in(key_list[9], 3), ROWS // ROWS_DEV)
    expert_ids = jax.vmap(lambda own, number: shared_out(jax.random.fold_in(key_list[9], 2), own, number, ROWS_DEV, EXPERTS, TOPK, CAP, 2))(expert_ids_keys, expert_ids_turns).reshape((ROWS, TOPK))
    expert_gates = jnp.clip(jnp.exp(jax.random.uniform(key_list[10], (ROWS, TOPK), jnp.float32, math.log(0.1), math.log(1.0))), 0.1, 1.0)
    norm_gain = jnp.clip(1.0 + 0.1 * jax.random.normal(key_list[11], (D,), jnp.float32), 0.5, 1.5).astype(jnp.bfloat16)
    w_gate = noise(key_list[12], (EXPERTS, D, EFF), D ** -0.5, 0.0625, ((0, 16), (2, 2)))
    w_up = noise(key_list[13], (EXPERTS, D, EFF), D ** -0.5, 0.0625, ((0, 16), (2, 2)))
    w_down = noise(key_list[14], (EXPERTS, EFF, D), EFF ** -0.5, 0.1875, ((0, 16), (1, 2)))
    return {"queries": queries, "resident_cache": resident_cache, "resident_len": resident_len, "new_cache": new_cache, "new_len": new_len, "new_owner": new_owner, "value_up": value_up, "w_output": w_output, "residual": residual, "expert_ids": expert_ids, "expert_gates": expert_gates, "norm_gain": norm_gain, "w_gate": w_gate, "w_up": w_up, "w_down": w_down}


def attend(queries, caches, length, value_up):
    inverse_root = (NOPE + ROPE) ** (-0.5)
    scores = jnp.einsum('rhc,rtc->rht', queries.astype(jnp.float32), caches.astype(jnp.float32)) * inverse_root
    inside = jnp.arange(caches.shape[1], dtype=jnp.int32)[None, None, :] < length[:, None, None]
    scores = jnp.where(inside, scores, -jnp.inf)
    highest = lax.optimization_barrier(jnp.max(scores, axis=2, keepdims=True))
    raised = jnp.exp(scores - highest)
    weights = (raised / lax.optimization_barrier(jnp.sum(raised, axis=2, keepdims=True))).astype(jnp.bfloat16)
    latent = jnp.einsum('rht,rtc->rhc', weights.astype(jnp.float32), caches[:, :, :LAT].astype(jnp.float32)).astype(jnp.bfloat16)
    values = jnp.einsum('rhc,hcv->rhv', latent.astype(jnp.float32), value_up.astype(jnp.float32)).astype(jnp.bfloat16)
    return values.reshape(values.shape[0], H * VDIM)

def reference(queries, resident_cache, resident_len, new_cache, new_len, new_owner, value_up, w_output, residual, expert_ids, expert_gates, norm_gain, w_gate, w_up, w_down):
    blocks = queries.reshape(N_EXPERT, ROWS_DEV, H, LAT + ROPE)
    ordering = jnp.argsort(new_owner, stable=True).astype(jnp.int32)
    resident_att = attend(blocks[:, :REQ_DEV].reshape(REQS, H, LAT + ROPE), resident_cache, resident_len, value_up)
    arrived_att = attend(blocks[:, REQ_DEV:].reshape(NEWS, H, LAT + ROPE), new_cache[ordering], new_len[ordering], value_up)
    attention = jnp.concatenate([resident_att.reshape(N_EXPERT, REQ_DEV, H * VDIM), arrived_att.reshape(N_EXPERT, NEW_DEV, H * VDIM)], axis=1).reshape(ROWS, H * VDIM)
    mixed = jnp.dot(attention, w_output, preferred_element_type=jnp.float32)
    hidden = (residual.astype(jnp.float32) + mixed).astype(jnp.bfloat16)
    picks = expert_ids.reshape(N_EXPERT, ROWS_DEV * TOPK)
    onehot = (picks[:, :, None] == jnp.arange(EXPERTS, dtype=jnp.int32)[None, None, :]).astype(jnp.int32)
    ranking = (lax.optimization_barrier(jnp.sum(jnp.cumsum(onehot, axis=1) * onehot, axis=2)) - 1).astype(jnp.int32)
    source = jnp.arange(N_EXPERT, dtype=jnp.int32)[:, None]
    slot_index = (picks * (N_EXPERT * CAP) + source * CAP + ranking).astype(jnp.int32)
    row_index = (source * ROWS_DEV + jnp.arange(ROWS_DEV * TOPK, dtype=jnp.int32)[None, :] // TOPK).astype(jnp.int32)
    slot_rows = jnp.full((EXPERTS * N_EXPERT * CAP,), ROWS, jnp.int32).at[slot_index.reshape(-1)].set(row_index.reshape(-1))
    padded = jnp.concatenate([hidden, jnp.zeros((1, D), jnp.bfloat16)], axis=0)
    inputs_all = padded[slot_rows].reshape(EXPERTS, N_EXPERT * CAP, D)

    def apply_expert(operands):
        inputs, gate_weight, up_weight, down_weight = operands
        values = inputs.astype(jnp.float32)
        inverse = lax.rsqrt(lax.optimization_barrier(jnp.mean(values * values, axis=1, keepdims=True)) + 1e-06)
        normed = (values * inverse * norm_gain.astype(jnp.float32)).astype(jnp.bfloat16)
        gate_act = jnp.dot(normed, gate_weight, preferred_element_type=jnp.float32)
        up_act = jnp.dot(normed, up_weight, preferred_element_type=jnp.float32)
        hidden_act = (jax.nn.silu(gate_act) * up_act).astype(jnp.bfloat16)
        return jnp.dot(hidden_act, down_weight, preferred_element_type=jnp.float32)
    expert_out = lax.map(apply_expert, (inputs_all, w_gate, w_up, w_down))
    picked = expert_out.reshape(EXPERTS * N_EXPERT * CAP, D)[slot_index.reshape(ROWS, TOPK)]
    routed = lax.optimization_barrier(jnp.sum(picked * expert_gates[:, :, None], axis=1))
    return (hidden.astype(jnp.float32) + routed).astype(jnp.bfloat16)
```

```python
import functools

import jax
import jax.numpy as jnp
from jax import lax
from jax.experimental import pallas as pl
from jax.experimental.pallas import tpu as pltpu
from jax.sharding import PartitionSpec as P

ROPE = 64
NOPE = 128
MESH = pl.DeviceIdType.MESH


def attend(queries, caches, length, value_up):
    inverse_root = (NOPE + ROPE) ** (-0.5)
    latent_width = value_up.shape[1]
    scores = (
        jnp.einsum("rhc,rtc->rht", queries, caches, preferred_element_type=jnp.float32)
        * inverse_root
    )
    inside = lax.broadcasted_iota(jnp.int32, scores.shape, 2) < length[:, None, None]
    scores = jnp.where(inside, scores, -jnp.inf)
    highest = jnp.max(scores, axis=2, keepdims=True)
    raised = jnp.exp(scores - highest)
    weights = (raised / jnp.sum(raised, axis=2, keepdims=True)).astype(jnp.bfloat16)
    latent = jnp.einsum(
        "rht,rtc->rhc", weights, caches[:, :, :latent_width], preferred_element_type=jnp.float32
    ).astype(jnp.bfloat16)
    values = jnp.einsum(
        "rhc,hcv->rhv", latent, value_up, preferred_element_type=jnp.float32
    ).astype(jnp.bfloat16)
    return values.reshape(values.shape[0], -1)


def earlier_equal(labels):
    count = labels.shape[0]
    position = jnp.arange(count, dtype=jnp.int32)
    before = (labels[:, None] == labels[None, :]) & (position[None, :] < position[:, None])
    return jnp.sum(before.astype(jnp.int32), axis=1)


class Place:
    def __init__(self, nz):
        self.nz = nz
        self.h = lax.axis_index("head")
        self.e = lax.axis_index("expert")
        self.z = self.e // 4
        self.y = (self.e // 2) % 2
        self.c = self.e % 2

    def at(self, z, y, c):
        return z * 4 + y * 2 + c

    def core(self):
        return (self.h, self.at(self.z, self.y, 1 - self.c))

    def across(self):
        return (self.h, self.at(self.z, 1 - self.y, self.c))

    def along(self, sign):
        return (self.h, self.at(self.z + sign, self.y, self.c))

    def other_head(self):
        return (1 - self.h, self.e)

    def inside(self, z):
        return (z >= 0) & (z < self.nz)


def greet(place):
    barrier = pltpu.get_barrier_semaphore()
    for target in (place.core(), place.across(), place.other_head()):
        pl.semaphore_signal(barrier, inc=1, device_id=target, device_id_type=MESH)
    for sign in (-1, 1):

        @pl.when(place.inside(place.z + sign))
        def _():
            pl.semaphore_signal(
                barrier, inc=1, device_id=place.along(sign), device_id_type=MESH
            )

    above = jnp.where(place.z < place.nz - 1, 1, 0)
    below = jnp.where(place.z > 0, 1, 0)
    pl.semaphore_wait(barrier, 3 + above + below)


def remote(src, dst, send, recv, target):
    return pltpu.make_async_remote_copy(
        src_ref=src,
        dst_ref=dst,
        send_sem=send,
        recv_sem=recv,
        device_id=target,
        device_id_type=MESH,
    )


def gather(place, view, parts, shared, sems):
    send_z, send_y, send_c, send_x, recv = sems
    nz = place.nz
    z, y, c = place.z, place.y, place.c
    me = (place.h, place.e)
    shared_slot = {}

    def each(fn):
        for index, part in enumerate(parts):
            fn(index, part)

    def copy(b, part, send, target):
        return remote(view(b, part), view(b, part), send, recv.at[b, part], target)

    def arrived(b, part):
        copy(b, part, send_c.at[0, 0, 0], me).wait_recv()

    def to_core(b, index, part, slot):
        copy(b, part, send_c.at[slot, b // 4, (b // 2) % 2], place.core()).start()

    def to_head(b, index, part):
        if index in shared:
            copy(b, part, send_x.at[b // 4, (b // 2) % 2], place.other_head()).start()

    def to_y(zz, index, part):
        copy(place.at(zz, y, c), part, send_y.at[index, zz], place.across()).start()

    def to_z(sign, zz, index, part):
        copy(place.at(zz, y, c), part, send_z.at[index, (sign + 1) // 2, zz], place.along(sign)).start()

    n = len(parts)
    other = [None] * n
    for index in shared:
        other[index] = parts[index] + 1 - 2 * place.h

    for index, part in enumerate(parts):
        for sign in (-1, 1):

            @pl.when(place.inside(z + sign))
            def _():
                to_z(sign, z, index, part)

        to_y(z, index, part)
        to_head(place.e, index, part)
        to_core(place.e, index, part, index)

    def from_z(d):
        for index, part in enumerate(parts):
            for sign in (-1, 1):
                zz = z - sign * d

                @pl.when(place.inside(zz))
                def _():
                    b = place.at(zz, y, c)
                    arrived(b, part)

                    @pl.when(place.inside(z + sign))
                    def _():
                        to_z(sign, zz, index, part)

                    to_y(zz, index, part)
                    to_head(b, index, part)
                    to_core(b, index, part, index)

    def at_distance(d, fn):
        if d == 0:
            fn(z)
            return
        for sign in (-1, 1):
            zz = z - sign * d

            @pl.when(place.inside(zz))
            def _():
                fn(zz)

    def from_y(d):
        for index, part in enumerate(parts):

            def one(zz):
                b = place.at(zz, 1 - y, c)
                arrived(b, part)
                to_head(b, index, part)
                to_core(b, index, part, index)

            at_distance(d, one)

    def from_head(d, yy):
        for k, index in enumerate(sorted(shared)):

            def one(zz):
                b = place.at(zz, yy, c)
                arrived(b, other[index])
                to_core(b, index, other[index], n + k)

            at_distance(d, one)

    for d in range(1, nz):
        from_z(d)
        from_y(d - 1)
        from_head(d - 1, y)
        if d > 1:
            from_head(d - 2, 1 - y)
    from_y(nz - 1)
    from_head(nz - 1, y)
    if nz > 1:
        from_head(nz - 2, 1 - y)
    from_head(nz - 1, 1 - y)

    for zz in range(nz):
        for yy in range(2):
            b = place.at(zz, yy, 1 - c)
            for part in parts:
                arrived(b, part)
            for index in sorted(shared):
                arrived(b, other[index])

    def settle():
        for index, part in enumerate(parts):
            for zz in range(nz):
                for sign in (-1, 1):
                    @pl.when(place.inside(z + sign) & ((z - zz) * sign >= 0))
                    def _():
                        copy(
                            place.at(zz, y, c),
                            part,
                            send_z.at[index, (sign + 1) // 2, zz],
                            me,
                        ).wait_send()

                copy(place.at(zz, y, c), part, send_y.at[index, zz], me).wait_send()
                for yy in range(2):
                    b = place.at(zz, yy, c)
                    if index in shared:
                        copy(b, part, send_x.at[zz, yy], me).wait_send()
                    copy(b, part, send_c.at[index, zz, yy], me).wait_send()
        for k, index in enumerate(sorted(shared)):
            for zz in range(nz):
                for yy in range(2):
                    b = place.at(zz, yy, c)
                    copy(b, other[index], send_c.at[n + k, zz, yy], me).wait_send()

    return settle


def layer(
    nz,
    plain_rows,
    att_ref,
    residual_ref,
    gain_ref,
    weight_ref,
    w_output,
    w_gate,
    w_up,
    w_down,
    out_ref,
    att,
    wo,
    wg,
    wu,
    wd,
    mixed,
    mixed_low,
    mixed_got,
    hidden,
    gate_acc,
    up_acc,
    act,
    partial,
    core_got,
    pair,
    across_low,
    across_got,
    chain_low,
    chain_got,
    head_low,
    head_got,
    col_low,
    col_got,
    load_sem,
    a_z,
    a_y,
    a_c,
    a_x,
    a_recv,
    m_send,
    m_recv,
    h_z,
    h_y,
    h_c,
    h_x,
    h_recv,
    rc_send,
    rc_recv,
    ry_send,
    ry_recv,
    rz_send,
    rz_recv,
    rx_send,
    rx_recv,
    rk_send,
    rk_recv,
):
    place = Place(nz)
    h, e, z, y, c = place.h, place.e, place.z, place.y, place.c
    rows_dev, inner = att_ref.shape
    rows, width = residual_ref.shape
    half = rows // 2
    quarter = rows // 4
    blocks = nz * 4
    me = (h, e)
    f32, bf16 = jnp.float32, jnp.bfloat16

    own = pltpu.make_async_copy(
        att_ref, att.at[pl.ds(pl.multiple_of(e * rows_dev, rows_dev), rows_dev), :], load_sem.at[4]
    )
    own.start()
    loads = [
        pltpu.make_async_copy(src, dst, load_sem.at[i])
        for i, (src, dst) in enumerate(((w_output, wo), (w_gate, wg), (w_up, wu), (w_down, wd)))
    ]
    for load in loads:
        load.start()
    greet(place)
    own.wait()

    def att_view(b, part):
        return att.at[
            pl.ds(pl.multiple_of(b * rows_dev, rows_dev), rows_dev),
            pl.ds(part * (inner // 2), inner // 2),
        ]

    settle_att = gather(place, att_view, [0, 1], (), (a_z, a_y, a_c, a_x, a_recv))

    loads[0].wait()
    mixed[...] = jnp.zeros_like(mixed)
    step = inner // 8

    def project(k, carry):
        at = pl.multiple_of(k * step, step)
        mixed[...] += lax.dot_general(
            att[:, pl.ds(at, step)],
            wo[:, pl.ds(at, step)],
            (((1,), (1,)), ((), ())),
            preferred_element_type=f32,
        )
        return carry

    lax.fori_loop(0, 8, project, 0)
    mixed_low[...] = mixed[...].astype(bf16)

    split_rows = (rows - plain_rows) // 2

    def part_rows(part):
        if isinstance(part, int) and part == 0:
            return pl.ds(0, plain_rows)
        return pl.ds(pl.multiple_of(plain_rows + (part - 1) * split_rows, 16), split_rows)

    exchange = []
    for index, (there, here) in enumerate(((0, 0), (2 - h, 1 + h))):
        out = remote(
            mixed_low.at[part_rows(there)],
            mixed_got.at[part_rows(there)],
            m_send.at[index],
            m_recv.at[index],
            place.other_head(),
        )
        out.start()
        exchange.append((out, here))
    for index, (out, here) in enumerate(exchange):
        remote(
            mixed_low.at[part_rows(here)],
            mixed_got.at[part_rows(here)],
            m_send.at[index],
            m_recv.at[index],
            me,
        ).wait_recv()
        at = part_rows(here)
        total = mixed_low[at, :].astype(f32) + mixed_got[at, :].astype(f32)
        hidden[e, at, :] = (residual_ref[at, :].astype(f32) + total).astype(bf16)

    def hidden_view(b, part):
        return hidden.at[b, part_rows(part)]

    settle_hidden = gather(place, hidden_view, [0, 1 + h], (1,), (h_z, h_y, h_c, h_x, h_recv))

    def square(b, total):
        values = hidden[b].astype(f32)
        return total + jnp.sum(values * values, axis=1, keepdims=True)

    squares = lax.fori_loop(0, blocks, square, jnp.zeros((rows, 1), f32))
    inverse = lax.rsqrt(squares * (1.0 / (blocks * width)) + 1e-06)
    loads[1].wait()
    loads[2].wait()
    gate_acc[...] = jnp.zeros_like(gate_acc)
    up_acc[...] = jnp.zeros_like(up_acc)

    def raise_up(b, carry):
        normed = (hidden[b].astype(f32) * inverse * gain_ref[b].astype(f32)).astype(bf16)
        at = pl.ds(pl.multiple_of(b * width, 64), width)
        gate_acc[...] += jnp.dot(normed, wg[at, :], preferred_element_type=f32)
        up_acc[...] += jnp.dot(normed, wu[at, :], preferred_element_type=f32)
        return carry

    lax.fori_loop(0, blocks, raise_up, 0)
    gate = gate_acc[...]
    act[...] = (jax.nn.silu(gate) * up_acc[...] * weight_ref[...]).astype(bf16)
    loads[3].wait()

    pair_width = 2 * width

    def down(zz, yy):
        q = zz * 2 + yy
        at = pl.ds(pl.multiple_of(q * pair_width, 128), pair_width)
        value = jnp.dot(act[...], wd[:, at], preferred_element_type=f32)
        partial[q] = value.astype(bf16).reshape(partial.shape[1:])
        remote(
            partial.at[q, :, 1 - c], core_got.at[q], rc_send.at[q], rc_recv.at[q], place.core()
        ).start()

    def join(zz, yy):
        q = zz * 2 + yy
        remote(
            partial.at[q, :, 1 - c], core_got.at[q], rc_send.at[q], rc_recv.at[q], me
        ).wait()
        return partial[q, :, c].astype(f32) + core_got[q].astype(f32)

    def cross(zz):
        across_low[zz] = join(zz, 1 - y).astype(bf16)
        remote(
            across_low.at[zz], across_got.at[zz], ry_send.at[zz], ry_recv.at[zz], place.across()
        ).start()

    def far_to_near(fn):
        for d in range(nz - 1, 0, -1):
            for sign in (-1, 1):
                zz = z + sign * d

                @pl.when(place.inside(zz))
                def _():
                    fn(zz, sign)

        fn(z, 0)

    far_to_near(lambda zz, sign: down(zz, 1 - y))

    def second(zz, sign):
        cross(zz)
        down(zz, y)

    far_to_near(second)

    def chain_copy(sign, zz, target):
        way = (sign + 1) // 2
        return remote(
            chain_low.at[way, zz],
            chain_got.at[way, zz],
            rz_send.at[way, zz],
            rz_recv.at[way, zz],
            target,
        )

    def merge(zz, sign):
        pair[...] = join(zz, y)
        remote(
            across_low.at[zz], across_got.at[zz], ry_send.at[zz], ry_recv.at[zz], me
        ).wait()
        pair[...] += across_got[zz].astype(f32)
        for way in (-1, 1) if sign == 0 else (sign,):

            @pl.when(place.inside(z - way))
            def _():
                chain_copy(way, zz, me).wait_recv()
                pair[...] += chain_got[(way + 1) // 2, zz].astype(f32)

        if sign != 0:
            chain_low[(sign + 1) // 2, zz] = pair[...].astype(bf16)
            chain_copy(sign, zz, place.along(sign)).start()

    far_to_near(merge)

    head_low[...] = pair[1 - h].astype(bf16)
    over = remote(head_low, head_got, rx_send, rx_recv, place.other_head())
    over.start()
    over.wait()
    total = pair[h] + head_got[...].astype(f32)
    left, right = total[:, :width], total[:, width:]
    mine = jnp.where(c == 0, left, right)
    col_low[...] = jnp.where(c == 0, right, left).astype(bf16)
    swap = remote(col_low, col_got, rk_send, rk_recv, place.core())
    swap.start()
    low = pl.multiple_of(c * quarter, quarter)
    start = pl.multiple_of(h * half + low, quarter)
    out_ref[pl.ds(low, quarter), :] = (
        hidden[e, pl.ds(start, quarter), :].astype(f32) + mine
    ).astype(out_ref.dtype)
    low = pl.multiple_of((1 - c) * quarter, quarter)
    start = pl.multiple_of(h * half + low, quarter)
    swap.wait()
    out_ref[pl.ds(low, quarter), :] = (
        hidden[e, pl.ds(start, quarter), :].astype(f32) + col_got[...].astype(f32)
    ).astype(out_ref.dtype)

    settle_att()
    for out, _ in exchange:
        out.wait_send()
    settle_hidden()
    for zz in range(nz):
        for sign in (-1, 1):

            @pl.when((zz - z) * sign > 0)
            def _():
                chain_copy(sign, zz, me).wait_send()


def fused_layer(nz, attention, w_output, residual, gain, weight, w_gate, w_up, w_down):
    rows_dev, inner = attention.shape
    rows, width = residual.shape
    d_model, hidden_units = w_gate.shape
    blocks = nz * 4
    quarter = rows // 4
    pair_width = 2 * width
    bf16, f32 = jnp.bfloat16, jnp.float32
    plain_rows = rows * 3 // 8
    dma = pltpu.SemaphoreType.DMA
    vmem = pl.BlockSpec(memory_space=pltpu.VMEM)
    hbm = pl.BlockSpec(memory_space=pl.ANY)
    block = (2, quarter, pair_width)
    return pl.pallas_call(
        functools.partial(layer, nz, plain_rows),
        out_shape=jax.ShapeDtypeStruct((rows // 2, width), bf16),
        in_specs=[vmem, vmem, vmem, vmem, hbm, hbm, hbm, hbm],
        out_specs=vmem,
        scratch_shapes=[
            pltpu.VMEM((rows, inner), bf16),
            pltpu.VMEM(w_output.shape, bf16),
            pltpu.VMEM(w_gate.shape, bf16),
            pltpu.VMEM(w_up.shape, bf16),
            pltpu.VMEM(w_down.shape, bf16),
            pltpu.VMEM((rows, width), f32),
            pltpu.VMEM((rows, width), bf16),
            pltpu.VMEM((rows, width), bf16),
            pltpu.VMEM((blocks, rows, width), bf16),
            pltpu.VMEM((rows, hidden_units), f32),
            pltpu.VMEM((rows, hidden_units), f32),
            pltpu.VMEM((rows, hidden_units), bf16),
            pltpu.VMEM((nz * 2, 2, 2, quarter, pair_width), bf16),
            pltpu.VMEM((nz * 2,) + block, bf16),
            pltpu.VMEM(block, f32),
            pltpu.VMEM((nz,) + block, bf16),
            pltpu.VMEM((nz,) + block, bf16),
            pltpu.VMEM((2, nz) + block, bf16),
            pltpu.VMEM((2, nz) + block, bf16),
            pltpu.VMEM(block[1:], bf16),
            pltpu.VMEM(block[1:], bf16),
            pltpu.VMEM((quarter, width), bf16),
            pltpu.VMEM((quarter, width), bf16),
            dma((5,)),
            dma((2, 2, nz)),
            dma((2, nz)),
            dma((2, nz, 2)),
            dma((1, 1)),
            dma((blocks, 2)),
            dma((2,)),
            dma((2,)),
            dma((2, 2, nz)),
            dma((2, nz)),
            dma((3, nz, 2)),
            dma((nz, 2)),
            dma((blocks, 3)),
            dma((nz * 2,)),
            dma((nz * 2,)),
            dma((nz,)),
            dma((nz,)),
            dma((2, nz)),
            dma((2, nz)),
            dma,
            dma,
            dma,
            dma,
        ],
        compiler_params=pltpu.CompilerParams(
            collective_id=0, has_side_effects=True, vmem_limit_bytes=62 * 2**20
        ),
        name="fused_layer",
    )(attention, residual, gain, weight, w_output, w_gate, w_up, w_down)


def per_device(
    queries,
    resident_cache,
    resident_len,
    new_cache,
    new_len,
    new_owner,
    value_up,
    w_output,
    residual,
    expert_ids,
    expert_gates,
    norm_gain,
    w_gate,
    w_up,
    w_down,
):
    n_expert = lax.axis_size("expert")
    n_head = lax.axis_size("head")
    owner_index = lax.axis_index("expert")
    head_index = lax.axis_index("head")
    req_count = resident_cache.shape[0]
    new_count, new_span, cache_width = new_cache.shape
    rows_dev = req_count + new_count
    rows_all = rows_dev * n_expert
    local_experts = w_gate.shape[0]
    most = max(2, (4 * new_count + 3 * n_expert - 1) // (3 * n_expert))
    block_rows = rows_all // n_head
    piece = new_span // n_head

    targets = lax.dynamic_slice_in_dim(new_owner, owner_index * new_count, new_count)
    places = targets * most + earlier_equal(targets)
    slots = jnp.arange(n_expert * most, dtype=jnp.int32)
    senders = jnp.sum(
        jnp.where(
            places[None, :] == slots[:, None], jnp.arange(new_count, dtype=jnp.int32)[None, :], 0
        ),
        axis=1,
    )
    share = lax.dynamic_slice_in_dim(new_cache, head_index * piece, piece, axis=1)
    outgoing = jnp.take(share, senders, axis=0, mode="clip").reshape(
        n_expert, most, piece, cache_width
    )
    incoming = lax.all_to_all(outgoing, "expert", split_axis=0, concat_axis=0, tiled=True)
    position = jnp.arange(new_owner.shape[0], dtype=jnp.int32)
    named = new_owner == owner_index
    before = jnp.sum((named[None, :] & (position[None, :] < position[:, None])).astype(jnp.int32), 1)
    chosen = jnp.sum(
        jnp.where(
            named[None, :]
            & (before[None, :] == jnp.arange(new_count, dtype=jnp.int32)[:, None]),
            position[None, :],
            0,
        ),
        axis=1,
    )
    anchor = chosen // new_count
    arrived_share = jnp.take(
        incoming.reshape(n_expert * most, piece, cache_width),
        anchor * most + earlier_equal(anchor),
        axis=0,
        mode="clip",
    )
    if n_head == 2:
        other = lax.ppermute(arrived_share, "head", [(0, 1), (1, 0)])
        first = jnp.where(head_index == 0, arrived_share, other)
        last = jnp.where(head_index == 0, other, arrived_share)
        arrived = jnp.concatenate([first, last], axis=1)
    else:
        arrived = lax.all_gather(arrived_share, "head", axis=1, tiled=True)
    resident_att = attend(queries[:req_count], resident_cache, resident_len, value_up)
    arrived_att = attend(queries[req_count:], arrived, new_len[chosen], value_up)
    attention = jnp.concatenate([resident_att, arrived_att], axis=0)

    if n_head == 2 and n_expert % 4 == 0 and local_experts == 1:
        mine = expert_ids == owner_index
        weight = jnp.sum(jnp.where(mine, expert_gates, 0.0), axis=1, keepdims=True)
        return fused_layer(
            n_expert // 4,
            attention,
            w_output.T,
            residual,
            norm_gain.reshape(n_expert, 1, -1),
            weight,
            w_gate[0],
            w_up[0],
            w_down[0],
        )

    mixed = jnp.dot(
        lax.all_gather(attention, "expert", axis=0, tiled=True),
        w_output,
        preferred_element_type=jnp.float32,
    ).T
    summed = lax.psum(mixed, "head")
    hidden = (residual.T.astype(jnp.float32) + summed).astype(jnp.bfloat16)
    hidden_block = lax.dynamic_slice_in_dim(hidden, head_index * block_rows, block_rows, axis=1)

    inputs = lax.all_gather(hidden, "expert", axis=0, tiled=True).astype(jnp.float32)
    inverse = lax.rsqrt(jnp.mean(inputs * inputs, axis=0, keepdims=True) + 1e-06)
    normed = (inputs * inverse * norm_gain.astype(jnp.float32)[:, None]).astype(jnp.bfloat16)
    partial = None
    for e in range(local_experts):
        gate_act = jnp.einsum("df,dr->fr", w_gate[e], normed, preferred_element_type=jnp.float32)
        up_act = jnp.einsum("df,dr->fr", w_up[e], normed, preferred_element_type=jnp.float32)
        act = (jax.nn.silu(gate_act) * up_act).astype(jnp.bfloat16)
        down = jnp.einsum("fd,fr->dr", w_down[e], act, preferred_element_type=jnp.float32)
        mine = expert_ids == owner_index * local_experts + e
        weight = jnp.sum(jnp.where(mine, expert_gates, 0.0), axis=1)
        term = down * weight[None, :]
        partial = term if partial is None else partial + term
    routed = lax.psum_scatter(
        partial.astype(jnp.bfloat16), "expert", scatter_dimension=0, tiled=True
    )
    routed_block = lax.psum_scatter(routed, "head", scatter_dimension=1, tiled=True).astype(
        jnp.float32
    )
    return (hidden_block.astype(jnp.float32) + routed_block).astype(jnp.bfloat16).T


def solution(mesh):
    return jax.shard_map(
        per_device,
        mesh=mesh,
        in_specs=(
            P("expert", "head", None),
            P("expert", None, None),
            P("expert"),
            P("expert", None, None),
            P(),
            P(),
            P("head", None, None),
            P("head", "expert"),
            P(None, "expert"),
            P(),
            P(),
            P(),
            P("expert", None, "head"),
            P("expert", None, "head"),
            P("expert", "head", None),
        ),
        out_specs=P("head", "expert"),
        check_vma=False,
    )
```

```python
import functools

import jax
import jax.numpy as jnp
from jax import lax
from jax.experimental import pallas as pl
from jax.experimental.pallas import tpu as pltpu
from jax.sharding import PartitionSpec as P

ROPE = 64
NOPE = 128
MESH = pl.DeviceIdType.MESH


def attend(queries, caches, length, value_up):
    inverse_root = (NOPE + ROPE) ** (-0.5)
    latent_width = value_up.shape[1]
    scores = (
        jnp.einsum("rhc,rtc->rht", queries, caches, preferred_element_type=jnp.float32)
        * inverse_root
    )
    inside = lax.broadcasted_iota(jnp.int32, scores.shape, 2) < length[:, None, None]
    scores = jnp.where(inside, scores, -jnp.inf)
    highest = jnp.max(scores, axis=2, keepdims=True)
    raised = jnp.exp(scores - highest)
    weights = (raised / jnp.sum(raised, axis=2, keepdims=True)).astype(jnp.bfloat16)
    latent = jnp.einsum(
        "rht,rtc->rhc", weights, caches[:, :, :latent_width], preferred_element_type=jnp.float32
    ).astype(jnp.bfloat16)
    return raise_values(latent, value_up)


def raise_values(latent, value_up):
    values = jnp.einsum(
        "rhc,hcv->rhv", latent, value_up, preferred_element_type=jnp.float32
    ).astype(jnp.bfloat16)
    return values.reshape(values.shape[0], -1)


def earlier_equal(labels):
    count = labels.shape[0]
    position = jnp.arange(count, dtype=jnp.int32)
    before = (labels[:, None] == labels[None, :]) & (position[None, :] < position[:, None])
    return jnp.sum(before.astype(jnp.int32), axis=1)


class Place:
    def __init__(self, nz):
        self.nz = nz
        self.h = lax.axis_index("head")
        self.e = lax.axis_index("expert")
        self.z = self.e // 4
        self.y = (self.e // 2) % 2
        self.c = self.e % 2

    def at(self, z, y, c):
        return z * 4 + y * 2 + c

    def core(self):
        return (self.h, self.at(self.z, self.y, 1 - self.c))

    def across(self):
        return (self.h, self.at(self.z, 1 - self.y, self.c))

    def along(self, sign):
        return (self.h, self.at(self.z + sign, self.y, self.c))

    def other_head(self):
        return (1 - self.h, self.e)

    def inside(self, z):
        return (z >= 0) & (z < self.nz)


def greet(place):
    barrier = pltpu.get_barrier_semaphore()
    for target in (place.core(), place.across(), place.other_head()):
        pl.semaphore_signal(barrier, inc=1, device_id=target, device_id_type=MESH)
    for sign in (-1, 1):

        @pl.when(place.inside(place.z + sign))
        def _():
            pl.semaphore_signal(
                barrier, inc=1, device_id=place.along(sign), device_id_type=MESH
            )

    above = jnp.where(place.z < place.nz - 1, 1, 0)
    below = jnp.where(place.z > 0, 1, 0)
    pl.semaphore_wait(barrier, 3 + above + below)


def remote(src, dst, send, recv, target):
    return pltpu.make_async_remote_copy(
        src_ref=src,
        dst_ref=dst,
        send_sem=send,
        recv_sem=recv,
        device_id=target,
        device_id_type=MESH,
    )


def gather(place, view, parts, shared, sems):
    send_z, send_y, send_c, send_x, recv = sems
    nz = place.nz
    z, y, c = place.z, place.y, place.c
    me = (place.h, place.e)
    shared_slot = {}

    def each(fn):
        for index, part in enumerate(parts):
            fn(index, part)

    def copy(b, part, send, target):
        return remote(view(b, part), view(b, part), send, recv.at[b, part], target)

    def arrived(b, part):
        copy(b, part, send_c.at[0, 0, 0], me).wait_recv()

    def to_core(b, index, part, slot):
        copy(b, part, send_c.at[slot, b // 4, (b // 2) % 2], place.core()).start()

    def to_head(b, index, part):
        if index in shared:
            copy(b, part, send_x.at[b // 4, (b // 2) % 2], place.other_head()).start()

    def to_y(zz, index, part):
        copy(place.at(zz, y, c), part, send_y.at[index, zz], place.across()).start()

    def to_z(sign, zz, index, part):
        copy(place.at(zz, y, c), part, send_z.at[index, (sign + 1) // 2, zz], place.along(sign)).start()

    n = len(parts)
    other = [None] * n
    for index in shared:
        other[index] = parts[index] + 1 - 2 * place.h

    for index, part in enumerate(parts):
        for sign in (-1, 1):

            @pl.when(place.inside(z + sign))
            def _():
                to_z(sign, z, index, part)

        to_y(z, index, part)
        to_head(place.e, index, part)
        to_core(place.e, index, part, index)

    def from_z(d):
        for index, part in enumerate(parts):
            for sign in (-1, 1):
                zz = z - sign * d

                @pl.when(place.inside(zz))
                def _():
                    b = place.at(zz, y, c)
                    arrived(b, part)

                    @pl.when(place.inside(z + sign))
                    def _():
                        to_z(sign, zz, index, part)

                    to_y(zz, index, part)
                    to_head(b, index, part)
                    to_core(b, index, part, index)

    def at_distance(d, fn):
        if d == 0:
            fn(z)
            return
        for sign in (-1, 1):
            zz = z - sign * d

            @pl.when(place.inside(zz))
            def _():
                fn(zz)

    def from_y(d):
        for index, part in enumerate(parts):

            def one(zz):
                b = place.at(zz, 1 - y, c)
                arrived(b, part)
                to_head(b, index, part)
                to_core(b, index, part, index)

            at_distance(d, one)

    def from_head(d, yy):
        for k, index in enumerate(sorted(shared)):

            def one(zz):
                b = place.at(zz, yy, c)
                arrived(b, other[index])
                to_core(b, index, other[index], n + k)

            at_distance(d, one)

    for d in range(1, nz):
        from_z(d)
        from_y(d - 1)
        from_head(d - 1, y)
        if d > 1:
            from_head(d - 2, 1 - y)
    from_y(nz - 1)
    from_head(nz - 1, y)
    if nz > 1:
        from_head(nz - 2, 1 - y)
    from_head(nz - 1, 1 - y)

    for zz in range(nz):
        for yy in range(2):
            b = place.at(zz, yy, 1 - c)
            for part in parts:
                arrived(b, part)
            for index in sorted(shared):
                arrived(b, other[index])

    def settle():
        for index, part in enumerate(parts):
            for zz in range(nz):
                for sign in (-1, 1):
                    @pl.when(place.inside(z + sign) & ((z - zz) * sign >= 0))
                    def _():
                        copy(
                            place.at(zz, y, c),
                            part,
                            send_z.at[index, (sign + 1) // 2, zz],
                            me,
                        ).wait_send()

                copy(place.at(zz, y, c), part, send_y.at[index, zz], me).wait_send()
                for yy in range(2):
                    b = place.at(zz, yy, c)
                    if index in shared:
                        copy(b, part, send_x.at[zz, yy], me).wait_send()
                    copy(b, part, send_c.at[index, zz, yy], me).wait_send()
        for k, index in enumerate(sorted(shared)):
            for zz in range(nz):
                for yy in range(2):
                    b = place.at(zz, yy, c)
                    copy(b, other[index], send_c.at[n + k, zz, yy], me).wait_send()

    return settle


def layer(
    nz,
    plain_rows,
    n_early,
    att_ref,
    residual_ref,
    gain_ref,
    ids_ref,
    gates_ref,
    w_output,
    w_gate,
    w_up,
    w_down,
    out_ref,
    att,
    wo,
    wg,
    wu,
    wd,
    base,
    mixed,
    mixed_low,
    mixed_got,
    hidden,
    gate_acc,
    up_acc,
    act,
    partial,
    core_got,
    joined,
    early_low,
    early_got,
    pair,
    across_low,
    across_got,
    chain_low,
    chain_got,
    head_low,
    head_got,
    col_low,
    col_got,
    load_sem,
    a_z,
    a_y,
    a_c,
    a_x,
    a_recv,
    m_send,
    m_recv,
    h_z,
    h_y,
    h_c,
    h_x,
    h_recv,
    rc_send,
    rc_recv,
    re_send,
    re_recv,
    ry_send,
    ry_recv,
    rz_send,
    rz_recv,
    rx_send,
    rx_recv,
    rk_send,
    rk_recv,
):
    place = Place(nz)
    h, e, z, y, c = place.h, place.e, place.z, place.y, place.c
    heads, rows_dev, value_width = att_ref.shape
    inner = heads * value_width
    width, rows = residual_ref.shape
    half = rows // 2
    quarter = rows // 4
    blocks = nz * 4
    me = (h, e)
    f32, bf16 = jnp.float32, jnp.bfloat16

    loads = [
        pltpu.make_async_copy(src, dst, load_sem.at[i])
        for i, (src, dst) in enumerate(((w_output, wo), (w_gate, wg), (w_up, wu), (w_down, wd)))
    ]
    for load in loads:
        load.start()
    own_rows = pl.ds(pl.multiple_of(e * rows_dev, rows_dev), rows_dev)
    for k in range(heads):
        att[own_rows, k * value_width : (k + 1) * value_width] = att_ref[k]
    greet(place)

    def att_view(b, part):
        return att.at[
            pl.ds(pl.multiple_of(b * rows_dev, rows_dev), rows_dev),
            pl.ds(part * (inner // 2), inner // 2),
        ]

    settle_att = gather(place, att_view, [0, 1], (), (a_z, a_y, a_c, a_x, a_recv))

    base[...] = residual_ref[...].astype(f32).T
    mine = jnp.where(ids_ref[...] == e, gates_ref[...], 0.0)
    weight = jnp.sum(mine.T, axis=1, keepdims=True)
    loads[0].wait()
    mixed[...] = jnp.zeros_like(mixed)
    step = inner // 8

    def project(k, carry):
        at = pl.multiple_of(k * step, step)
        mixed[...] += lax.dot_general(
            att[:, pl.ds(at, step)],
            wo[:, pl.ds(at, step)],
            (((1,), (1,)), ((), ())),
            preferred_element_type=f32,
        )
        return carry

    lax.fori_loop(0, 8, project, 0)
    mixed_low[...] = mixed[...].astype(bf16)

    split_rows = (rows - plain_rows) // 2

    def part_rows(part):
        if isinstance(part, int) and part == 0:
            return pl.ds(0, plain_rows)
        return pl.ds(pl.multiple_of(plain_rows + (part - 1) * split_rows, 16), split_rows)

    exchange = []
    for index, (there, here) in enumerate(((0, 0), (2 - h, 1 + h))):
        out = remote(
            mixed_low.at[part_rows(there)],
            mixed_got.at[part_rows(there)],
            m_send.at[index],
            m_recv.at[index],
            place.other_head(),
        )
        out.start()
        exchange.append((out, here))
    for index, (out, here) in enumerate(exchange):
        remote(
            mixed_low.at[part_rows(here)],
            mixed_got.at[part_rows(here)],
            m_send.at[index],
            m_recv.at[index],
            me,
        ).wait_recv()
        at = part_rows(here)
        total = mixed_low[at, :].astype(f32) + mixed_got[at, :].astype(f32)
        hidden[e, at, :] = (base[at, :] + total).astype(bf16)

    def hidden_view(b, part):
        return hidden.at[b, part_rows(part)]

    settle_hidden = gather(place, hidden_view, [0, 1 + h], (1,), (h_z, h_y, h_c, h_x, h_recv))

    def square(b, total):
        values = hidden[b].astype(f32)
        return total + jnp.sum(values * values, axis=1, keepdims=True)

    squares = lax.fori_loop(0, blocks, square, jnp.zeros((rows, 1), f32))
    inverse = lax.rsqrt(squares * (1.0 / (blocks * width)) + 1e-06)
    loads[1].wait()
    loads[2].wait()
    gate_acc[...] = jnp.zeros_like(gate_acc)
    up_acc[...] = jnp.zeros_like(up_acc)

    def raise_up(b, carry):
        normed = (hidden[b].astype(f32) * inverse * gain_ref[b].astype(f32)).astype(bf16)
        at = pl.ds(pl.multiple_of(b * width, 64), width)
        gate_acc[...] += jnp.dot(normed, wg[at, :], preferred_element_type=f32)
        up_acc[...] += jnp.dot(normed, wu[at, :], preferred_element_type=f32)
        return carry

    lax.fori_loop(0, blocks, raise_up, 0)
    gate = gate_acc[...]
    act[...] = (jax.nn.silu(gate) * up_acc[...] * weight).astype(bf16)
    loads[3].wait()

    pair_width = 2 * width
    early, late = pl.ds(0, n_early), pl.ds(n_early, joined.shape[1] - n_early)
    n_late = quarter - n_early

    def down(zz, yy):
        q = zz * 2 + yy
        at = pl.ds(pl.multiple_of(q * pair_width, 128), pair_width)
        value = jnp.dot(act[...], wd[:, at], preferred_element_type=f32)
        partial[q] = value.astype(bf16).reshape(partial.shape[1:])
        core_copy(q, place.core()).start()

    def core_copy(q, target):
        return remote(
            partial.at[q, :, 1 - c], core_got.at[q], rc_send.at[q], rc_recv.at[q], target
        )

    def early_copy(q, target):
        return remote(early_low.at[q], early_got.at[q], re_send.at[q], re_recv.at[q], target)

    def across_copy(zz, k, target):
        at = (early, late)[k]
        return remote(
            across_low.at[zz, at],
            across_got.at[zz, at],
            ry_send.at[zz, k],
            ry_recv.at[zz, k],
            target,
        )

    def chain_copy(sign, zz, k, target):
        way, at = (sign + 1) // 2, (early, late)[k]
        return remote(
            chain_low.at[way, zz, at],
            chain_got.at[way, zz, at],
            rz_send.at[way, zz, k],
            rz_recv.at[way, zz, k],
            target,
        )

    def at_distance(d, fn):
        if d == 0:
            fn(z, 0)
            return
        for sign in (-1, 1):
            zz = z + sign * d

            @pl.when(place.inside(zz))
            def _():
                fn(zz, sign)

    def both_down(zz, sign):
        down(zz, 1 - y)
        down(zz, y)

    def join(zz, sign):
        for k, yy in enumerate((1 - y, y)):
            q = zz * 2 + yy
            core_copy(q, me).wait()

            def total(head, at):
                return partial[q, head, c, at].astype(f32) + core_got[q, head, at].astype(f32)

            early_low[q] = total(1 - h, early).astype(bf16)
            early_copy(q, place.other_head()).start()
            joined[q, early] = total(h, early)
            rest = [total(head, pl.ds(n_early, n_late)) for head in range(2)]
            if k == 0:
                across_low[zz, late] = jnp.concatenate(rest, axis=0).astype(bf16)
                across_copy(zz, 1, place.across()).start()
            else:
                joined[q, late] = jnp.concatenate(rest, axis=0)

    def cross(zz, sign):
        q = zz * 2 + 1 - y
        early_copy(q, me).wait()
        across_low[zz, early] = (joined[q, early] + early_got[q].astype(f32)).astype(bf16)
        across_copy(zz, 0, place.across()).start()

    def merge(zz, sign):
        q = zz * 2 + y
        pair[...] = joined[q]
        for k in (1, 0):
            at = (early, late)[k]
            if k == 0:
                early_copy(q, me).wait()
                pair[at, :] += early_got[q].astype(f32)
            across_copy(zz, k, me).wait()
            pair[at, :] += across_got[zz, at].astype(f32)
            for way in (-1, 1) if sign == 0 else (sign,):

                @pl.when(place.inside(z - way))
                def _():
                    chain_copy(way, zz, k, me).wait_recv()
                    pair[at, :] += chain_got[(way + 1) // 2, zz, at].astype(f32)

            if sign != 0:
                chain_low[(sign + 1) // 2, zz, at] = pair[at, :].astype(bf16)
                chain_copy(sign, zz, k, place.along(sign)).start()

    for d in range(nz - 1, -1, -1):
        at_distance(d, both_down)
    for d in range(nz - 1, -1, -1):
        at_distance(d, join)
    at_distance(nz - 1, cross)
    for d in range(nz - 1, -1, -1):
        if d > 0:
            at_distance(d - 1, cross)
        at_distance(d, merge)

    def late_rows(head):
        return pl.ds(pl.multiple_of(n_early + head * n_late, 16), n_late)

    head_low[...] = pair[late_rows(1 - h), :].astype(bf16)
    over = remote(head_low, head_got, rx_send, rx_recv, place.other_head())
    over.start()
    over.wait()
    total = jnp.concatenate(
        [pair[early, :], pair[late_rows(h), :] + head_got[...].astype(f32)], axis=0
    )
    left, right = total[:, :width], total[:, width:]
    mine = jnp.where(c == 0, left, right)
    col_low[...] = jnp.where(c == 0, right, left).astype(bf16)
    swap = remote(col_low, col_got, rk_send, rk_recv, place.core())
    swap.start()
    low = pl.multiple_of(c * quarter, quarter)
    start = pl.multiple_of(h * half + low, quarter)
    out_ref[pl.ds(low, quarter), :] = (
        hidden[e, pl.ds(start, quarter), :].astype(f32) + mine
    ).astype(out_ref.dtype)
    low = pl.multiple_of((1 - c) * quarter, quarter)
    start = pl.multiple_of(h * half + low, quarter)
    swap.wait()
    out_ref[pl.ds(low, quarter), :] = (
        hidden[e, pl.ds(start, quarter), :].astype(f32) + col_got[...].astype(f32)
    ).astype(out_ref.dtype)

    settle_att()
    for out, _ in exchange:
        out.wait_send()
    settle_hidden()
    for zz in range(nz):
        for sign in (-1, 1):

            @pl.when((zz - z) * sign > 0)
            def _():
                for k in range(2):
                    chain_copy(sign, zz, k, me).wait_send()


def fused_layer(nz, attention, w_output, residual, gain, ids, gates, w_gate, w_up, w_down):
    heads, rows_dev, value_width = attention.shape
    inner = heads * value_width
    width, rows = residual.shape
    d_model, hidden_units = w_gate.shape
    blocks = nz * 4
    quarter = rows // 4
    pair_width = 2 * width
    bf16, f32 = jnp.bfloat16, jnp.float32
    plain_rows = rows * 3 // 8
    dma = pltpu.SemaphoreType.DMA
    vmem = pl.BlockSpec(memory_space=pltpu.VMEM)
    hbm = pl.BlockSpec(memory_space=pl.ANY)
    n_early = quarter * 3 // 4 // 16 * 16
    kept = (2 * quarter - n_early, pair_width)
    early = (nz * 2, n_early, pair_width)
    return pl.pallas_call(
        functools.partial(layer, nz, plain_rows, n_early),
        out_shape=jax.ShapeDtypeStruct((rows // 2, width), bf16),
        in_specs=[vmem, vmem, vmem, vmem, vmem, hbm, hbm, hbm, hbm],
        out_specs=vmem,
        scratch_shapes=[
            pltpu.VMEM((rows, inner), bf16),
            pltpu.VMEM(w_output.shape, bf16),
            pltpu.VMEM(w_gate.shape, bf16),
            pltpu.VMEM(w_up.shape, bf16),
            pltpu.VMEM(w_down.shape, bf16),
            pltpu.VMEM((rows, width), f32),
            pltpu.VMEM((rows, width), f32),
            pltpu.VMEM((rows, width), bf16),
            pltpu.VMEM((rows, width), bf16),
            pltpu.VMEM((blocks, rows, width), bf16),
            pltpu.VMEM((rows, hidden_units), f32),
            pltpu.VMEM((rows, hidden_units), f32),
            pltpu.VMEM((rows, hidden_units), bf16),
            pltpu.VMEM((nz * 2, 2, 2, quarter, pair_width), bf16),
            pltpu.VMEM((nz * 2, 2, quarter, pair_width), bf16),
            pltpu.VMEM((nz * 2,) + kept, f32),
            pltpu.VMEM(early, bf16),
            pltpu.VMEM(early, bf16),
            pltpu.VMEM(kept, f32),
            pltpu.VMEM((nz,) + kept, bf16),
            pltpu.VMEM((nz,) + kept, bf16),
            pltpu.VMEM((2, nz) + kept, bf16),
            pltpu.VMEM((2, nz) + kept, bf16),
            pltpu.VMEM((quarter - n_early, pair_width), bf16),
            pltpu.VMEM((quarter - n_early, pair_width), bf16),
            pltpu.VMEM((quarter, width), bf16),
            pltpu.VMEM((quarter, width), bf16),
            dma((4,)),
            dma((2, 2, nz)),
            dma((2, nz)),
            dma((2, nz, 2)),
            dma((1, 1)),
            dma((blocks, 2)),
            dma((2,)),
            dma((2,)),
            dma((2, 2, nz)),
            dma((2, nz)),
            dma((3, nz, 2)),
            dma((nz, 2)),
            dma((blocks, 3)),
            dma((nz * 2,)),
            dma((nz * 2,)),
            dma((nz * 2,)),
            dma((nz * 2,)),
            dma((nz, 2)),
            dma((nz, 2)),
            dma((2, nz, 2)),
            dma((2, nz, 2)),
            dma,
            dma,
            dma,
            dma,
        ],
        compiler_params=pltpu.CompilerParams(
            collective_id=0, has_side_effects=True, vmem_limit_bytes=62 * 2**20
        ),
        name="fused_layer",
    )(attention, residual, gain, ids, gates, w_output, w_gate, w_up, w_down)


def weigh(scores, length):
    inverse_root = (NOPE + ROPE) ** (-0.5)
    inside = lax.broadcasted_iota(jnp.int32, scores.shape, 1) < length
    scores = jnp.where(inside, scores * inverse_root, -jnp.inf)
    raised = jnp.exp(scores - jnp.max(scores, axis=1, keepdims=True))
    return (raised / jnp.sum(raised, axis=1, keepdims=True)).astype(jnp.bfloat16)


def score(queries, cache):
    return lax.dot_general(
        queries, cache, (((1,), (1,)), ((), ())), preferred_element_type=jnp.float32
    )


def handoff(
    nz,
    most,
    cache_hbm,
    queries_hbm,
    resident_hbm,
    resident_len,
    senders,
    slot,
    new_len,
    latent_ref,
    cache_ref,
    outgoing_ref,
    queries_ref,
    resident_ref,
    got,
    scores,
    load_sem,
    own_sem,
    send,
    recv,
    pass_send,
    pass_recv,
):
    place = Place(nz)
    h, e = place.h, place.e
    count = nz * 4
    loads = [
        pltpu.make_async_copy(src, dst, load_sem.at[i])
        for i, (src, dst) in enumerate(
            ((cache_hbm, cache_ref), (queries_hbm, queries_ref), (resident_hbm, resident_ref))
        )
    ]
    for load in loads:
        load.start()
    req_count = resident_ref.shape[0]
    new_count = slot.shape[0]
    width = latent_ref.shape[2]
    me = (h, e)

    half = nz // 2
    low = (place.z // half) * half
    order = [
        (side, dz, dy, dc)
        for side in (1, 0)
        for dz in reversed(range(half))
        for dy in (1, 0)
        for dc in (1, 0)
    ][: count - 1]

    def partner(sign, side, dz, dy, dc):
        base = low if side == 0 else (nz - half) - low
        z = base + lax.rem(place.z - low + half + sign * dz, half)
        return place.at(z, (place.y + dy) % 2, (place.c + dc) % 2)

    def target(*step):
        return partner(1, *step)

    def source(*step):
        return partner(-1, *step)

    def unit(ref, b, head=None):
        at = pl.ds(b * most, most)
        return ref.at[at] if head is None else ref.at[at, head]

    def positions(step):
        return h if step[0] == 1 else None

    def sent(index, there, target_id):
        part = positions(order[index])
        return remote(
            unit(outgoing_ref, there, part), unit(got, e, part), send.at[index], recv.at[e], target_id
        )

    barrier = pltpu.get_barrier_semaphore()
    pl.semaphore_signal(barrier, inc=1, device_id=place.other_head(), device_id_type=MESH)
    for step in order:
        pl.semaphore_signal(
            barrier, inc=1, device_id=(h, target(*step)), device_id_type=MESH
        )
    loads[0].wait()
    for k in range(count * most):
        outgoing_ref[k] = cache_ref[senders[k]]
    own = pltpu.make_async_copy(unit(outgoing_ref, e), unit(got, e), own_sem)
    own.start()
    pl.semaphore_wait(barrier, count)

    for index, step in enumerate(order):
        there = target(*step)
        sent(index, there, (h, there)).start()

    def arrived(step, b):
        part = positions(step)
        remote(
            unit(outgoing_ref, b, part), unit(got, b, part), send.at[0], recv.at[b], me
        ).wait_recv()

    def passed(index, b, head, target_id):
        return remote(
            unit(got, b, head), unit(got, b, head), pass_send.at[index], pass_recv.at[b], target_id
        )

    def resident(r):
        scores_r = jnp.dot(queries_ref[r], resident_ref[r], preferred_element_type=jnp.float32)
        weights = weigh(scores_r, resident_len[r])
        latent_ref[r] = score(weights, resident_ref[r, :width, :]).astype(latent_ref.dtype)

    own.wait()
    loads[1].wait()
    loads[2].wait()
    crossing = [i for i in range(count - 1) if order[i][0] == 1]
    inside = [i for i in range(count - 1) if order[i][0] == 0]
    done = 0
    for k, index in enumerate(crossing):
        b = source(*order[index])
        arrived(order[index], b)
        passed(index, b, h, place.other_head()).start()
        if k % 2 == 1 and done < req_count:
            resident(done)
            done += 1
    for r in range(done, req_count):
        resident(r)
    for index in inside:
        arrived(order[index], source(*order[index]))
    for index in crossing:
        b = source(*order[index])
        passed(index, b, 1 - h, me).wait_recv()

    def cache_of(j):
        cache = got[slot[j]]
        return cache.reshape(cache.shape[0] * cache.shape[1], cache.shape[2])

    for j in range(new_count):
        scores[j] = score(queries_ref[req_count + j], cache_of(j))
    for j in range(new_count):
        weights = weigh(scores[j], new_len[j])
        latent_ref[req_count + j] = jnp.dot(
            weights, cache_of(j)[:, :width], preferred_element_type=jnp.float32
        ).astype(latent_ref.dtype)

    for index, step in enumerate(order):
        sent(index, target(*step), me).wait_send()
    for index in crossing:
        passed(index, source(*order[index]), h, me).wait_send()


def latents(nz, most, cache, queries, resident, resident_len, senders, slot, new_len, width):
    new_count, halves, piece, cache_width = cache.shape
    rows, heads, _ = queries.shape
    slots = senders.shape[0]
    count = nz * 4
    dma = pltpu.SemaphoreType.DMA
    hbm = pl.BlockSpec(memory_space=pl.ANY)
    smem = pl.BlockSpec(memory_space=pltpu.SMEM)
    return pl.pallas_call(
        functools.partial(handoff, nz, most),
        out_shape=jax.ShapeDtypeStruct((rows, heads, width), jnp.bfloat16),
        in_specs=[hbm, hbm, hbm, smem, smem, smem, smem],
        out_specs=pl.BlockSpec(memory_space=pltpu.VMEM),
        scratch_shapes=[
            pltpu.VMEM(cache.shape, jnp.bfloat16),
            pltpu.VMEM((slots,) + cache.shape[1:], jnp.bfloat16),
            pltpu.VMEM(queries.shape, jnp.bfloat16),
            pltpu.VMEM(resident.shape, jnp.bfloat16),
            pltpu.VMEM((slots,) + cache.shape[1:], jnp.bfloat16),
            pltpu.VMEM((new_count, heads, halves * piece), jnp.float32),
            dma((3,)),
            dma,
            dma((count,)),
            dma((count,)),
            dma((count,)),
            dma((count,)),
        ],
        compiler_params=pltpu.CompilerParams(
            collective_id=1, has_side_effects=True, vmem_limit_bytes=62 * 2**20
        ),
        name="handoff",
    )(cache, queries, resident, resident_len, senders, slot, new_len)


def per_device(
    queries,
    resident_cache,
    resident_len,
    new_cache,
    new_len,
    new_owner,
    value_up,
    w_output,
    residual,
    expert_ids,
    expert_gates,
    norm_gain,
    w_gate,
    w_up,
    w_down,
):
    n_expert = lax.axis_size("expert")
    n_head = lax.axis_size("head")
    owner_index = lax.axis_index("expert")
    head_index = lax.axis_index("head")
    req_count = resident_cache.shape[0]
    new_count, new_span, cache_width = new_cache.shape
    rows_dev = req_count + new_count
    rows_all = rows_dev * n_expert
    local_experts = w_gate.shape[0]
    most = max(2, (4 * new_count + 3 * n_expert - 1) // (3 * n_expert))
    block_rows = rows_all // n_head
    piece = new_span // n_head

    targets = lax.dynamic_slice_in_dim(new_owner, owner_index * new_count, new_count)
    places = targets * most + earlier_equal(targets)
    slots = jnp.arange(n_expert * most, dtype=jnp.int32)
    senders = jnp.sum(
        jnp.where(
            places[None, :] == slots[:, None], jnp.arange(new_count, dtype=jnp.int32)[None, :], 0
        ),
        axis=1,
    )
    position = jnp.arange(new_owner.shape[0], dtype=jnp.int32)
    named = new_owner == owner_index
    before = jnp.sum((named[None, :] & (position[None, :] < position[:, None])).astype(jnp.int32), 1)
    taken = named[None, :] & (
        before[None, :] == jnp.arange(new_count, dtype=jnp.int32)[:, None]
    )
    chosen = jnp.sum(jnp.where(taken, position[None, :], 0), axis=1)
    anchor = chosen // new_count
    slot = anchor * most + earlier_equal(anchor)
    lengths = jnp.sum(jnp.where(taken, new_len[None, :], 0), axis=1)

    if n_head == 2 and n_expert % 8 == 0 and local_experts == 1:
        latent = latents(
            n_expert // 4,
            most,
            new_cache.reshape(new_count, n_head, piece, cache_width),
            queries,
            jnp.swapaxes(resident_cache, 1, 2),
            resident_len,
            senders,
            slot,
            lengths,
            value_up.shape[1],
        )
        attention = jnp.einsum(
            "rhc,hcv->hrv", latent, value_up, preferred_element_type=jnp.float32
        ).astype(jnp.bfloat16)
        return fused_layer(
            n_expert // 4,
            attention,
            w_output.T,
            residual.T,
            norm_gain.reshape(n_expert, 1, -1),
            expert_ids.T,
            expert_gates.T,
            w_gate[0],
            w_up[0],
            w_down[0],
        )

    share = lax.dynamic_slice_in_dim(new_cache, head_index * piece, piece, axis=1)
    outgoing = jnp.take(share, senders, axis=0, mode="clip").reshape(
        n_expert, most, piece, cache_width
    )
    incoming = lax.all_to_all(outgoing, "expert", split_axis=0, concat_axis=0, tiled=True)
    arrived_share = jnp.take(
        incoming.reshape(n_expert * most, piece, cache_width), slot, axis=0, mode="clip"
    )
    arrived = lax.all_gather(arrived_share, "head", axis=1, tiled=True)
    resident_att = attend(queries[:req_count], resident_cache, resident_len, value_up)
    arrived_att = attend(queries[req_count:], arrived, lengths, value_up)
    attention = jnp.concatenate([resident_att, arrived_att], axis=0)
    mixed = jnp.dot(
        lax.all_gather(attention, "expert", axis=0, tiled=True),
        w_output,
        preferred_element_type=jnp.float32,
    ).T
    summed = lax.psum(mixed, "head")
    hidden = (residual.T.astype(jnp.float32) + summed).astype(jnp.bfloat16)
    hidden_block = lax.dynamic_slice_in_dim(hidden, head_index * block_rows, block_rows, axis=1)

    inputs = lax.all_gather(hidden, "expert", axis=0, tiled=True).astype(jnp.float32)
    inverse = lax.rsqrt(jnp.mean(inputs * inputs, axis=0, keepdims=True) + 1e-06)
    normed = (inputs * inverse * norm_gain.astype(jnp.float32)[:, None]).astype(jnp.bfloat16)
    partial = None
    for e in range(local_experts):
        gate_act = jnp.einsum("df,dr->fr", w_gate[e], normed, preferred_element_type=jnp.float32)
        up_act = jnp.einsum("df,dr->fr", w_up[e], normed, preferred_element_type=jnp.float32)
        act = (jax.nn.silu(gate_act) * up_act).astype(jnp.bfloat16)
        down = jnp.einsum("fd,fr->dr", w_down[e], act, preferred_element_type=jnp.float32)
        mine = expert_ids == owner_index * local_experts + e
        weight = jnp.sum(jnp.where(mine, expert_gates, 0.0), axis=1)
        term = down * weight[None, :]
        partial = term if partial is None else partial + term
    routed = lax.psum_scatter(
        partial.astype(jnp.bfloat16), "expert", scatter_dimension=0, tiled=True
    )
    routed_block = lax.psum_scatter(routed, "head", scatter_dimension=1, tiled=True).astype(
        jnp.float32
    )
    return (hidden_block.astype(jnp.float32) + routed_block).astype(jnp.bfloat16).T


def solution(mesh):
    return jax.shard_map(
        per_device,
        mesh=mesh,
        in_specs=(
            P("expert", "head", None),
            P("expert", None, None),
            P("expert"),
            P("expert", None, None),
            P(),
            P(),
            P("head", None, None),
            P("head", "expert"),
            P(None, "expert"),
            P(),
            P(),
            P(),
            P("expert", None, "head"),
            P("expert", None, "head"),
            P("expert", "head", None),
        ),
        out_specs=P("head", "expert"),
        check_vma=False,
    )
```

```python
import functools

import jax
import jax.numpy as jnp
from jax import lax
from jax.experimental import pallas as pl
from jax.experimental.pallas import tpu as pltpu
from jax.sharding import PartitionSpec as P

ROPE = 64
NOPE = 128
MESH = pl.DeviceIdType.MESH


def attend(queries, caches, length, value_up):
    inverse_root = (NOPE + ROPE) ** (-0.5)
    latent_width = value_up.shape[1]
    scores = (
        jnp.einsum("rhc,rtc->rht", queries, caches, preferred_element_type=jnp.float32)
        * inverse_root
    )
    inside = lax.broadcasted_iota(jnp.int32, scores.shape, 2) < length[:, None, None]
    scores = jnp.where(inside, scores, -jnp.inf)
    highest = jnp.max(scores, axis=2, keepdims=True)
    raised = jnp.exp(scores - highest)
    weights = (raised / jnp.sum(raised, axis=2, keepdims=True)).astype(jnp.bfloat16)
    latent = jnp.einsum(
        "rht,rtc->rhc", weights, caches[:, :, :latent_width], preferred_element_type=jnp.float32
    ).astype(jnp.bfloat16)
    return raise_values(latent, value_up)


def raise_values(latent, value_up):
    values = jnp.einsum(
        "rhc,hcv->rhv", latent, value_up, preferred_element_type=jnp.float32
    ).astype(jnp.bfloat16)
    return values.reshape(values.shape[0], -1)


def earlier_equal(labels):
    count = labels.shape[0]
    position = jnp.arange(count, dtype=jnp.int32)
    before = (labels[:, None] == labels[None, :]) & (position[None, :] < position[:, None])
    return jnp.sum(before.astype(jnp.int32), axis=1)


class Place:
    def __init__(self, nz):
        self.nz = nz
        self.h = lax.axis_index("head")
        self.e = lax.axis_index("expert")
        self.z = self.e // 4
        self.y = (self.e // 2) % 2
        self.c = self.e % 2

    def at(self, z, y, c):
        return z * 4 + y * 2 + c

    def core(self):
        return (self.h, self.at(self.z, self.y, 1 - self.c))

    def across(self):
        return (self.h, self.at(self.z, 1 - self.y, self.c))

    def along(self, sign):
        return (self.h, self.at(self.z + sign, self.y, self.c))

    def other_head(self):
        return (1 - self.h, self.e)

    def inside(self, z):
        return (z >= 0) & (z < self.nz)


def greet(place):
    barrier = pltpu.get_barrier_semaphore()
    for target in (place.core(), place.across(), place.other_head()):
        pl.semaphore_signal(barrier, inc=1, device_id=target, device_id_type=MESH)
    for sign in (-1, 1):

        @pl.when(place.inside(place.z + sign))
        def _():
            pl.semaphore_signal(
                barrier, inc=1, device_id=place.along(sign), device_id_type=MESH
            )

    above = jnp.where(place.z < place.nz - 1, 1, 0)
    below = jnp.where(place.z > 0, 1, 0)
    pl.semaphore_wait(barrier, 3 + above + below)


def remote(src, dst, send, recv, target):
    return pltpu.make_async_remote_copy(
        src_ref=src,
        dst_ref=dst,
        send_sem=send,
        recv_sem=recv,
        device_id=target,
        device_id_type=MESH,
    )


def gather(place, view, parts, shared, sems):
    send_z, send_y, send_c, send_x, recv = sems
    nz = place.nz
    z, y, c = place.z, place.y, place.c
    me = (place.h, place.e)
    shared_slot = {}

    def each(fn):
        for index, part in enumerate(parts):
            fn(index, part)

    def copy(b, part, send, target):
        return remote(view(b, part), view(b, part), send, recv.at[b, part], target)

    def arrived(b, part):
        copy(b, part, send_c.at[0, 0, 0], me).wait_recv()

    def to_core(b, index, part, slot):
        copy(b, part, send_c.at[slot, b // 4, (b // 2) % 2], place.core()).start()

    def to_head(b, index, part):
        if index in shared:
            copy(b, part, send_x.at[b // 4, (b // 2) % 2], place.other_head()).start()

    def to_y(zz, index, part):
        copy(place.at(zz, y, c), part, send_y.at[index, zz], place.across()).start()

    def to_z(sign, zz, index, part):
        copy(place.at(zz, y, c), part, send_z.at[index, (sign + 1) // 2, zz], place.along(sign)).start()

    n = len(parts)
    other = [None] * n
    for index in shared:
        other[index] = parts[index] + 1 - 2 * place.h

    for index, part in enumerate(parts):
        for sign in (-1, 1):

            @pl.when(place.inside(z + sign))
            def _():
                to_z(sign, z, index, part)

        to_y(z, index, part)
        to_head(place.e, index, part)
        to_core(place.e, index, part, index)

    def from_z(d):
        for index, part in enumerate(parts):
            for sign in (-1, 1):
                zz = z - sign * d

                @pl.when(place.inside(zz))
                def _():
                    b = place.at(zz, y, c)
                    arrived(b, part)

                    @pl.when(place.inside(z + sign))
                    def _():
                        to_z(sign, zz, index, part)

                    to_y(zz, index, part)
                    to_head(b, index, part)
                    to_core(b, index, part, index)

    def at_distance(d, fn):
        if d == 0:
            fn(z)
            return
        for sign in (-1, 1):
            zz = z - sign * d

            @pl.when(place.inside(zz))
            def _():
                fn(zz)

    def from_y(d):
        for index, part in enumerate(parts):

            def one(zz):
                b = place.at(zz, 1 - y, c)
                arrived(b, part)
                to_head(b, index, part)
                to_core(b, index, part, index)

            at_distance(d, one)

    def from_head(d, yy):
        for k, index in enumerate(sorted(shared)):

            def one(zz):
                b = place.at(zz, yy, c)
                arrived(b, other[index])
                to_core(b, index, other[index], n + k)

            at_distance(d, one)

    for d in range(1, nz):
        from_z(d)
        from_y(d - 1)
        from_head(d - 1, y)
        if d > 1:
            from_head(d - 2, 1 - y)
    from_y(nz - 1)
    from_head(nz - 1, y)
    if nz > 1:
        from_head(nz - 2, 1 - y)
    from_head(nz - 1, 1 - y)

    for zz in range(nz):
        for yy in range(2):
            b = place.at(zz, yy, 1 - c)
            for part in parts:
                arrived(b, part)
            for index in sorted(shared):
                arrived(b, other[index])

    def settle():
        for index, part in enumerate(parts):
            for zz in range(nz):
                for sign in (-1, 1):
                    @pl.when(place.inside(z + sign) & ((z - zz) * sign >= 0))
                    def _():
                        copy(
                            place.at(zz, y, c),
                            part,
                            send_z.at[index, (sign + 1) // 2, zz],
                            me,
                        ).wait_send()

                copy(place.at(zz, y, c), part, send_y.at[index, zz], me).wait_send()
                for yy in range(2):
                    b = place.at(zz, yy, c)
                    if index in shared:
                        copy(b, part, send_x.at[zz, yy], me).wait_send()
                    copy(b, part, send_c.at[index, zz, yy], me).wait_send()
        for k, index in enumerate(sorted(shared)):
            for zz in range(nz):
                for yy in range(2):
                    b = place.at(zz, yy, c)
                    copy(b, other[index], send_c.at[n + k, zz, yy], me).wait_send()

    return settle


def layer(
    nz,
    plain_rows,
    n_early,
    att_ref,
    residual_ref,
    gain_ref,
    ids_ref,
    gates_ref,
    w_output,
    w_gate,
    w_up,
    w_down,
    out_ref,
    att,
    wo,
    wg,
    wu,
    wd,
    base,
    mixed,
    mixed_low,
    mixed_got,
    hidden,
    gate_acc,
    up_acc,
    act,
    partial,
    core_got,
    joined,
    early_low,
    early_got,
    pair,
    across_low,
    across_got,
    chain_low,
    chain_got,
    head_low,
    head_got,
    col_low,
    col_got,
    load_sem,
    a_z,
    a_y,
    a_c,
    a_x,
    a_recv,
    m_send,
    m_recv,
    h_z,
    h_y,
    h_c,
    h_x,
    h_recv,
    rc_send,
    rc_recv,
    re_send,
    re_recv,
    ry_send,
    ry_recv,
    rz_send,
    rz_recv,
    rx_send,
    rx_recv,
    rk_send,
    rk_recv,
):
    place = Place(nz)
    h, e, z, y, c = place.h, place.e, place.z, place.y, place.c
    heads, rows_dev, value_width = att_ref.shape
    inner = heads * value_width
    width, rows = residual_ref.shape
    half = rows // 2
    quarter = rows // 4
    blocks = nz * 4
    me = (h, e)
    f32, bf16 = jnp.float32, jnp.bfloat16

    loads = [
        pltpu.make_async_copy(src, dst, load_sem.at[i])
        for i, (src, dst) in enumerate(((w_output, wo), (w_gate, wg), (w_up, wu), (w_down, wd)))
    ]
    for load in loads:
        load.start()
    own_rows = pl.ds(pl.multiple_of(e * rows_dev, rows_dev), rows_dev)
    for k in range(heads):
        att[own_rows, k * value_width : (k + 1) * value_width] = att_ref[k]
    greet(place)

    def att_view(b, part):
        return att.at[
            pl.ds(pl.multiple_of(b * rows_dev, rows_dev), rows_dev),
            pl.ds(part * (inner // 2), inner // 2),
        ]

    settle_att = gather(place, att_view, [0, 1], (), (a_z, a_y, a_c, a_x, a_recv))

    base[...] = residual_ref[...].astype(f32).T
    mine = jnp.where(ids_ref[...] == e, gates_ref[...], 0.0)
    weight = jnp.sum(mine.T, axis=1, keepdims=True)
    loads[0].wait()
    mixed[...] = jnp.zeros_like(mixed)
    step = inner // 8

    def project(k, carry):
        at = pl.multiple_of(k * step, step)
        mixed[...] += lax.dot_general(
            att[:, pl.ds(at, step)],
            wo[:, pl.ds(at, step)],
            (((1,), (1,)), ((), ())),
            preferred_element_type=f32,
        )
        return carry

    lax.fori_loop(0, 8, project, 0)
    mixed_low[...] = mixed[...].astype(bf16)

    split_rows = (rows - plain_rows) // 2

    def part_rows(part):
        if isinstance(part, int) and part == 0:
            return pl.ds(0, plain_rows)
        return pl.ds(pl.multiple_of(plain_rows + (part - 1) * split_rows, 16), split_rows)

    exchange = []
    for index, (there, here) in enumerate(((0, 0), (2 - h, 1 + h))):
        out = remote(
            mixed_low.at[part_rows(there)],
            mixed_got.at[part_rows(there)],
            m_send.at[index],
            m_recv.at[index],
            place.other_head(),
        )
        out.start()
        exchange.append((out, here))
    for index, (out, here) in enumerate(exchange):
        remote(
            mixed_low.at[part_rows(here)],
            mixed_got.at[part_rows(here)],
            m_send.at[index],
            m_recv.at[index],
            me,
        ).wait_recv()
        at = part_rows(here)
        total = mixed_low[at, :].astype(f32) + mixed_got[at, :].astype(f32)
        hidden[e, at, :] = (base[at, :] + total).astype(bf16)

    def hidden_view(b, part):
        return hidden.at[b, part_rows(part)]

    settle_hidden = gather(place, hidden_view, [0, 1 + h], (1,), (h_z, h_y, h_c, h_x, h_recv))

    loads[1].wait()
    loads[2].wait()
    gate_acc[...] = jnp.zeros_like(gate_acc)
    up_acc[...] = jnp.zeros_like(up_acc)

    def raise_up(b, squares):
        values = hidden[b].astype(f32)
        scaled = (values * gain_ref[b].astype(f32)).astype(bf16)
        at = pl.ds(pl.multiple_of(b * width, 64), width)
        gate_acc[...] += jnp.dot(scaled, wg[at, :], preferred_element_type=f32)
        up_acc[...] += jnp.dot(scaled, wu[at, :], preferred_element_type=f32)
        return squares + jnp.sum(values * values, axis=1, keepdims=True)

    squares = lax.fori_loop(0, blocks, raise_up, jnp.zeros((rows, 1), f32))
    inverse = lax.rsqrt(squares * (1.0 / (blocks * width)) + 1e-06)
    gate = gate_acc[...] * inverse
    act[...] = (jax.nn.silu(gate) * up_acc[...] * (inverse * weight)).astype(bf16)
    loads[3].wait()

    pair_width = 2 * width
    early, late = pl.ds(0, n_early), pl.ds(n_early, joined.shape[1] - n_early)
    n_late = quarter - n_early

    def down(zz, yy):
        q = zz * 2 + yy
        at = pl.ds(pl.multiple_of(q * pair_width, 128), pair_width)
        value = jnp.dot(act[...], wd[:, at], preferred_element_type=f32)
        partial[q] = value.astype(bf16).reshape(partial.shape[1:])
        core_copy(q, place.core()).start()

    def core_copy(q, target):
        return remote(
            partial.at[q, :, 1 - c], core_got.at[q], rc_send.at[q], rc_recv.at[q], target
        )

    def early_copy(q, target):
        return remote(early_low.at[q], early_got.at[q], re_send.at[q], re_recv.at[q], target)

    def across_copy(zz, k, target):
        at = (early, late)[k]
        return remote(
            across_low.at[zz, at],
            across_got.at[zz, at],
            ry_send.at[zz, k],
            ry_recv.at[zz, k],
            target,
        )

    def chain_copy(sign, zz, k, target):
        way, at = (sign + 1) // 2, (early, late)[k]
        return remote(
            chain_low.at[way, zz, at],
            chain_got.at[way, zz, at],
            rz_send.at[way, zz, k],
            rz_recv.at[way, zz, k],
            target,
        )

    def at_distance(d, fn):
        if d == 0:
            fn(z, 0)
            return
        for sign in (-1, 1):
            zz = z + sign * d

            @pl.when(place.inside(zz))
            def _():
                fn(zz, sign)

    def both_down(zz, sign):
        down(zz, 1 - y)
        down(zz, y)

    def join(zz, sign):
        for k, yy in enumerate((1 - y, y)):
            q = zz * 2 + yy
            core_copy(q, me).wait()

            def total(head, at):
                return partial[q, head, c, at].astype(f32) + core_got[q, head, at].astype(f32)

            early_low[q] = total(1 - h, early).astype(bf16)
            early_copy(q, place.other_head()).start()
            joined[q, early] = total(h, early)
            rest = [total(head, pl.ds(n_early, n_late)) for head in range(2)]
            if k == 0:
                across_low[zz, late] = jnp.concatenate(rest, axis=0).astype(bf16)
                across_copy(zz, 1, place.across()).start()
            else:
                joined[q, late] = jnp.concatenate(rest, axis=0)

    def cross(zz, sign):
        q = zz * 2 + 1 - y
        early_copy(q, me).wait()
        across_low[zz, early] = (joined[q, early] + early_got[q].astype(f32)).astype(bf16)
        across_copy(zz, 0, place.across()).start()

    def merge(zz, sign):
        q = zz * 2 + y
        pair[...] = joined[q]
        for k in (1, 0):
            at = (early, late)[k]
            if k == 0:
                early_copy(q, me).wait()
                pair[at, :] += early_got[q].astype(f32)
            across_copy(zz, k, me).wait()
            pair[at, :] += across_got[zz, at].astype(f32)
            for way in (-1, 1) if sign == 0 else (sign,):

                @pl.when(place.inside(z - way))
                def _():
                    chain_copy(way, zz, k, me).wait_recv()
                    pair[at, :] += chain_got[(way + 1) // 2, zz, at].astype(f32)

            if sign != 0:
                chain_low[(sign + 1) // 2, zz, at] = pair[at, :].astype(bf16)
                chain_copy(sign, zz, k, place.along(sign)).start()

    for d in range(nz - 1, -1, -1):
        at_distance(d, both_down)
    for d in range(nz - 1, -1, -1):
        at_distance(d, join)
    at_distance(nz - 1, cross)
    for d in range(nz - 1, -1, -1):
        if d > 0:
            at_distance(d - 1, cross)
        at_distance(d, merge)

    def late_rows(head):
        return pl.ds(pl.multiple_of(n_early + head * n_late, 16), n_late)

    head_low[...] = pair[late_rows(1 - h), :].astype(bf16)
    over = remote(head_low, head_got, rx_send, rx_recv, place.other_head())
    over.start()
    over.wait()
    total = jnp.concatenate(
        [pair[early, :], pair[late_rows(h), :] + head_got[...].astype(f32)], axis=0
    )
    left, right = total[:, :width], total[:, width:]
    mine = jnp.where(c == 0, left, right)
    col_low[...] = jnp.where(c == 0, right, left).astype(bf16)
    swap = remote(col_low, col_got, rk_send, rk_recv, place.core())
    swap.start()
    low = pl.multiple_of(c * quarter, quarter)
    start = pl.multiple_of(h * half + low, quarter)
    out_ref[pl.ds(low, quarter), :] = (
        hidden[e, pl.ds(start, quarter), :].astype(f32) + mine
    ).astype(out_ref.dtype)
    low = pl.multiple_of((1 - c) * quarter, quarter)
    start = pl.multiple_of(h * half + low, quarter)
    swap.wait()
    out_ref[pl.ds(low, quarter), :] = (
        hidden[e, pl.ds(start, quarter), :].astype(f32) + col_got[...].astype(f32)
    ).astype(out_ref.dtype)

    settle_att()
    for out, _ in exchange:
        out.wait_send()
    settle_hidden()
    for zz in range(nz):
        for sign in (-1, 1):

            @pl.when((zz - z) * sign > 0)
            def _():
                for k in range(2):
                    chain_copy(sign, zz, k, me).wait_send()


def fused_layer(nz, attention, w_output, residual, gain, ids, gates, w_gate, w_up, w_down):
    heads, rows_dev, value_width = attention.shape
    inner = heads * value_width
    width, rows = residual.shape
    d_model, hidden_units = w_gate.shape
    blocks = nz * 4
    quarter = rows // 4
    pair_width = 2 * width
    bf16, f32 = jnp.bfloat16, jnp.float32
    plain_rows = rows * 3 // 8
    dma = pltpu.SemaphoreType.DMA
    vmem = pl.BlockSpec(memory_space=pltpu.VMEM)
    hbm = pl.BlockSpec(memory_space=pl.ANY)
    n_early = quarter * 3 // 4 // 16 * 16
    kept = (2 * quarter - n_early, pair_width)
    early = (nz * 2, n_early, pair_width)
    return pl.pallas_call(
        functools.partial(layer, nz, plain_rows, n_early),
        out_shape=jax.ShapeDtypeStruct((rows // 2, width), bf16),
        in_specs=[vmem, vmem, vmem, vmem, vmem, hbm, hbm, hbm, hbm],
        out_specs=vmem,
        scratch_shapes=[
            pltpu.VMEM((rows, inner), bf16),
            pltpu.VMEM(w_output.shape, bf16),
            pltpu.VMEM(w_gate.shape, bf16),
            pltpu.VMEM(w_up.shape, bf16),
            pltpu.VMEM(w_down.shape, bf16),
            pltpu.VMEM((rows, width), f32),
            pltpu.VMEM((rows, width), f32),
            pltpu.VMEM((rows, width), bf16),
            pltpu.VMEM((rows, width), bf16),
            pltpu.VMEM((blocks, rows, width), bf16),
            pltpu.VMEM((rows, hidden_units), f32),
            pltpu.VMEM((rows, hidden_units), f32),
            pltpu.VMEM((rows, hidden_units), bf16),
            pltpu.VMEM((nz * 2, 2, 2, quarter, pair_width), bf16),
            pltpu.VMEM((nz * 2, 2, quarter, pair_width), bf16),
            pltpu.VMEM((nz * 2,) + kept, f32),
            pltpu.VMEM(early, bf16),
            pltpu.VMEM(early, bf16),
            pltpu.VMEM(kept, f32),
            pltpu.VMEM((nz,) + kept, bf16),
            pltpu.VMEM((nz,) + kept, bf16),
            pltpu.VMEM((2, nz) + kept, bf16),
            pltpu.VMEM((2, nz) + kept, bf16),
            pltpu.VMEM((quarter - n_early, pair_width), bf16),
            pltpu.VMEM((quarter - n_early, pair_width), bf16),
            pltpu.VMEM((quarter, width), bf16),
            pltpu.VMEM((quarter, width), bf16),
            dma((4,)),
            dma((2, 2, nz)),
            dma((2, nz)),
            dma((2, nz, 2)),
            dma((1, 1)),
            dma((blocks, 2)),
            dma((2,)),
            dma((2,)),
            dma((2, 2, nz)),
            dma((2, nz)),
            dma((3, nz, 2)),
            dma((nz, 2)),
            dma((blocks, 3)),
            dma((nz * 2,)),
            dma((nz * 2,)),
            dma((nz * 2,)),
            dma((nz * 2,)),
            dma((nz, 2)),
            dma((nz, 2)),
            dma((2, nz, 2)),
            dma((2, nz, 2)),
            dma,
            dma,
            dma,
            dma,
        ],
        compiler_params=pltpu.CompilerParams(
            collective_id=0, has_side_effects=True, vmem_limit_bytes=62 * 2**20
        ),
        name="fused_layer",
    )(attention, residual, gain, ids, gates, w_output, w_gate, w_up, w_down)


def weigh(scores, length):
    inverse_root = (NOPE + ROPE) ** (-0.5)
    inside = lax.broadcasted_iota(jnp.int32, scores.shape, 1) < length
    scores = jnp.where(inside, scores * inverse_root, -jnp.inf)
    raised = jnp.exp(scores - jnp.max(scores, axis=1, keepdims=True))
    return (raised / jnp.sum(raised, axis=1, keepdims=True)).astype(jnp.bfloat16)


def score(queries, cache):
    return lax.dot_general(
        queries, cache, (((1,), (1,)), ((), ())), preferred_element_type=jnp.float32
    )


def handoff(
    nz,
    most,
    cache_hbm,
    queries_hbm,
    resident_hbm,
    resident_len,
    senders,
    slot,
    new_len,
    latent_ref,
    cache_ref,
    outgoing_ref,
    outgoing_tail,
    queries_ref,
    resident_ref,
    got,
    got_tail,
    scores,
    load_sem,
    own_sem,
    send,
    recv,
    pass_send,
    pass_recv,
):
    place = Place(nz)
    h, e = place.h, place.e
    count = nz * 4
    loads = [
        pltpu.make_async_copy(src, dst, load_sem.at[i])
        for i, (src, dst) in enumerate(
            ((cache_hbm, cache_ref), (queries_hbm, queries_ref), (resident_hbm, resident_ref))
        )
    ]
    for load in loads:
        load.start()
    req_count = resident_ref.shape[0]
    new_count = slot.shape[0]
    width = latent_ref.shape[2]
    me = (h, e)

    half = nz // 2
    low = (place.z // half) * half
    order = [
        (side, dz, dy, dc)
        for side in (1, 0)
        for dz in reversed(range(half))
        for dy in (1, 0)
        for dc in (1, 0)
    ][: count - 1]

    def partner(sign, side, dz, dy, dc):
        base = low if side == 0 else (nz - half) - low
        z = base + lax.rem(place.z - low + half + sign * dz, half)
        return place.at(z, (place.y + dy) % 2, (place.c + dc) % 2)

    def target(*step):
        return partner(1, *step)

    def source(*step):
        return partner(-1, *step)

    def unit(ref, b, head=None):
        at = pl.ds(b * most, most)
        return ref.at[at] if head is None else ref.at[at, head]

    def positions(step):
        return h if step[0] == 1 else None

    def tail(ref, b, head=None):
        return ref.at[b] if head is None else ref.at[b, head]

    def sent(index, there, target_id):
        part = positions(order[index])
        return [
            remote(
                view(src, there, part), view(dst, e, part), send.at[k, index], recv.at[k, e], target_id
            )
            for k, (view, src, dst) in enumerate(
                ((unit, outgoing_ref, got), (tail, outgoing_tail, got_tail))
            )
        ]

    barrier = pltpu.get_barrier_semaphore()
    pl.semaphore_signal(barrier, inc=1, device_id=place.other_head(), device_id_type=MESH)
    for step in order:
        pl.semaphore_signal(
            barrier, inc=1, device_id=(h, target(*step)), device_id_type=MESH
        )
    loads[0].wait()
    for b in range(count):
        caches = [cache_ref[senders[b * most + k]] for k in range(most)]
        for k in range(most):
            outgoing_ref[b * most + k] = caches[k][:, :, :width]
        outgoing_tail[b] = jnp.concatenate([cache[:, :, width:] for cache in caches], axis=2)
    own = [
        pltpu.make_async_copy(unit(outgoing_ref, e), unit(got, e), own_sem.at[0]),
        pltpu.make_async_copy(outgoing_tail.at[e], got_tail.at[e], own_sem.at[1]),
    ]
    for copy in own:
        copy.start()
    pl.semaphore_wait(barrier, count)

    for index, step in enumerate(order):
        there = target(*step)
        for copy in sent(index, there, (h, there)):
            copy.start()

    def arrived(step, b):
        part = positions(step)
        for k, (view, ref) in enumerate(((unit, got), (tail, got_tail))):
            at = view(ref, b, part)
            remote(at, at, send.at[k, 0], recv.at[k, b], me).wait_recv()

    def passed(index, b, head, target_id):
        return [
            remote(
                view(ref, b, head),
                view(ref, b, head),
                pass_send.at[k, index],
                pass_recv.at[k, b],
                target_id,
            )
            for k, (view, ref) in enumerate(((unit, got), (tail, got_tail)))
        ]

    def resident(r):
        scores_r = jnp.dot(queries_ref[r], resident_ref[r], preferred_element_type=jnp.float32)
        weights = weigh(scores_r, resident_len[r])
        latent_ref[r] = score(weights, resident_ref[r, :width, :]).astype(latent_ref.dtype)

    for copy in own:
        copy.wait()
    loads[1].wait()
    loads[2].wait()
    crossing = [i for i in range(count - 1) if order[i][0] == 1]
    inside = [i for i in range(count - 1) if order[i][0] == 0]
    done = 0
    for k, index in enumerate(crossing):
        b = source(*order[index])
        arrived(order[index], b)
        for copy in passed(index, b, h, place.other_head()):
            copy.start()
        if k % 2 == 1 and done < req_count:
            resident(done)
            done += 1
    for r in range(done, req_count):
        resident(r)
    for index in inside:
        arrived(order[index], source(*order[index]))
    for index in crossing:
        b = source(*order[index])
        for copy in passed(index, b, 1 - h, me):
            copy.wait_recv()

    def flat(cache):
        return cache.reshape(cache.shape[0] * cache.shape[1], cache.shape[2])

    def cache_of(j):
        return flat(got[slot[j]])

    def tail_of(j):
        tails = flat(got_tail[slot[j] // most])
        length = tails.shape[1] // most
        chosen = tails[:, :length]
        for k in range(1, most):
            chosen = jnp.where(slot[j] % most == k, tails[:, k * length : (k + 1) * length], chosen)
        return chosen

    for j in range(new_count):
        own_queries = queries_ref[req_count + j]
        scores[j] = score(own_queries[:, :width], cache_of(j)) + score(
            own_queries[:, width:], tail_of(j)
        )
    for j in range(new_count):
        weights = weigh(scores[j], new_len[j])
        latent_ref[req_count + j] = jnp.dot(
            weights, cache_of(j), preferred_element_type=jnp.float32
        ).astype(latent_ref.dtype)

    for index, step in enumerate(order):
        for copy in sent(index, target(*step), me):
            copy.wait_send()
    for index in crossing:
        for copy in passed(index, source(*order[index]), h, me):
            copy.wait_send()


def latents(nz, most, cache, queries, resident, resident_len, senders, slot, new_len, width):
    new_count, halves, piece, cache_width = cache.shape
    rows, heads, _ = queries.shape
    slots = senders.shape[0]
    count = nz * 4
    dma = pltpu.SemaphoreType.DMA
    hbm = pl.BlockSpec(memory_space=pl.ANY)
    smem = pl.BlockSpec(memory_space=pltpu.SMEM)
    return pl.pallas_call(
        functools.partial(handoff, nz, most),
        out_shape=jax.ShapeDtypeStruct((rows, heads, width), jnp.bfloat16),
        in_specs=[hbm, hbm, hbm, smem, smem, smem, smem],
        out_specs=pl.BlockSpec(memory_space=pltpu.VMEM),
        scratch_shapes=[
            pltpu.VMEM(cache.shape, jnp.bfloat16),
            pltpu.VMEM((slots, halves, piece, width), jnp.bfloat16),
            pltpu.VMEM((count, halves, piece, most * (cache_width - width)), jnp.bfloat16),
            pltpu.VMEM(queries.shape, jnp.bfloat16),
            pltpu.VMEM(resident.shape, jnp.bfloat16),
            pltpu.VMEM((slots, halves, piece, width), jnp.bfloat16),
            pltpu.VMEM((count, halves, piece, most * (cache_width - width)), jnp.bfloat16),
            pltpu.VMEM((new_count, heads, halves * piece), jnp.float32),
            dma((3,)),
            dma((2,)),
            dma((2, count)),
            dma((2, count)),
            dma((2, count)),
            dma((2, count)),
        ],
        compiler_params=pltpu.CompilerParams(
            collective_id=1, has_side_effects=True, vmem_limit_bytes=62 * 2**20
        ),
        name="handoff",
    )(cache, queries, resident, resident_len, senders, slot, new_len)


def per_device(
    queries,
    resident_cache,
    resident_len,
    new_cache,
    new_len,
    new_owner,
    value_up,
    w_output,
    residual,
    expert_ids,
    expert_gates,
    norm_gain,
    w_gate,
    w_up,
    w_down,
):
    n_expert = lax.axis_size("expert")
    n_head = lax.axis_size("head")
    owner_index = lax.axis_index("expert")
    head_index = lax.axis_index("head")
    req_count = resident_cache.shape[0]
    new_count, new_span, cache_width = new_cache.shape
    rows_dev = req_count + new_count
    rows_all = rows_dev * n_expert
    local_experts = w_gate.shape[0]
    most = max(2, (4 * new_count + 3 * n_expert - 1) // (3 * n_expert))
    block_rows = rows_all // n_head
    piece = new_span // n_head

    targets = lax.dynamic_slice_in_dim(new_owner, owner_index * new_count, new_count)
    places = targets * most + earlier_equal(targets)
    slots = jnp.arange(n_expert * most, dtype=jnp.int32)
    senders = jnp.sum(
        jnp.where(
            places[None, :] == slots[:, None], jnp.arange(new_count, dtype=jnp.int32)[None, :], 0
        ),
        axis=1,
    )
    position = jnp.arange(new_owner.shape[0], dtype=jnp.int32)
    named = new_owner == owner_index
    before = jnp.sum((named[None, :] & (position[None, :] < position[:, None])).astype(jnp.int32), 1)
    taken = named[None, :] & (
        before[None, :] == jnp.arange(new_count, dtype=jnp.int32)[:, None]
    )
    chosen = jnp.sum(jnp.where(taken, position[None, :], 0), axis=1)
    anchor = chosen // new_count
    slot = anchor * most + earlier_equal(anchor)
    lengths = jnp.sum(jnp.where(taken, new_len[None, :], 0), axis=1)

    if n_head == 2 and n_expert % 8 == 0 and local_experts == 1:
        latent = latents(
            n_expert // 4,
            most,
            new_cache.reshape(new_count, n_head, piece, cache_width),
            queries,
            jnp.swapaxes(resident_cache, 1, 2),
            resident_len,
            senders,
            slot,
            lengths,
            value_up.shape[1],
        )
        attention = jnp.einsum(
            "rhc,hcv->hrv", latent, value_up, preferred_element_type=jnp.float32
        ).astype(jnp.bfloat16)
        return fused_layer(
            n_expert // 4,
            attention,
            w_output.T,
            residual.T,
            norm_gain.reshape(n_expert, 1, -1),
            expert_ids.T,
            expert_gates.T,
            w_gate[0],
            w_up[0],
            w_down[0],
        )

    share = lax.dynamic_slice_in_dim(new_cache, head_index * piece, piece, axis=1)
    outgoing = jnp.take(share, senders, axis=0, mode="clip").reshape(
        n_expert, most, piece, cache_width
    )
    incoming = lax.all_to_all(outgoing, "expert", split_axis=0, concat_axis=0, tiled=True)
    arrived_share = jnp.take(
        incoming.reshape(n_expert * most, piece, cache_width), slot, axis=0, mode="clip"
    )
    arrived = lax.all_gather(arrived_share, "head", axis=1, tiled=True)
    resident_att = attend(queries[:req_count], resident_cache, resident_len, value_up)
    arrived_att = attend(queries[req_count:], arrived, lengths, value_up)
    attention = jnp.concatenate([resident_att, arrived_att], axis=0)
    mixed = jnp.dot(
        lax.all_gather(attention, "expert", axis=0, tiled=True),
        w_output,
        preferred_element_type=jnp.float32,
    ).T
    summed = lax.psum(mixed, "head")
    hidden = (residual.T.astype(jnp.float32) + summed).astype(jnp.bfloat16)
    hidden_block = lax.dynamic_slice_in_dim(hidden, head_index * block_rows, block_rows, axis=1)

    inputs = lax.all_gather(hidden, "expert", axis=0, tiled=True).astype(jnp.float32)
    inverse = lax.rsqrt(jnp.mean(inputs * inputs, axis=0, keepdims=True) + 1e-06)
    normed = (inputs * inverse * norm_gain.astype(jnp.float32)[:, None]).astype(jnp.bfloat16)
    partial = None
    for e in range(local_experts):
        gate_act = jnp.einsum("df,dr->fr", w_gate[e], normed, preferred_element_type=jnp.float32)
        up_act = jnp.einsum("df,dr->fr", w_up[e], normed, preferred_element_type=jnp.float32)
        act = (jax.nn.silu(gate_act) * up_act).astype(jnp.bfloat16)
        down = jnp.einsum("fd,fr->dr", w_down[e], act, preferred_element_type=jnp.float32)
        mine = expert_ids == owner_index * local_experts + e
        weight = jnp.sum(jnp.where(mine, expert_gates, 0.0), axis=1)
        term = down * weight[None, :]
        partial = term if partial is None else partial + term
    routed = lax.psum_scatter(
        partial.astype(jnp.bfloat16), "expert", scatter_dimension=0, tiled=True
    )
    routed_block = lax.psum_scatter(routed, "head", scatter_dimension=1, tiled=True).astype(
        jnp.float32
    )
    return (hidden_block.astype(jnp.float32) + routed_block).astype(jnp.bfloat16).T


def solution(mesh):
    return jax.shard_map(
        per_device,
        mesh=mesh,
        in_specs=(
            P("expert", "head", None),
            P("expert", None, None),
            P("expert"),
            P("expert", None, None),
            P(),
            P(),
            P("head", None, None),
            P("head", "expert"),
            P(None, "expert"),
            P(),
            P(),
            P(),
            P("expert", None, "head"),
            P("expert", None, "head"),
            P("expert", "head", None),
        ),
        out_specs=P("head", "expert"),
        check_vma=False,
    )
```
